32 devices in a mesh: shots: 2 (over y), wide: 16 (over z, x, core).
Axes of the slice: x: 2, y: 2, z: 4, core: 2. Of those that a mesh axis runs over, the one named last changes fastest.
Arguments:
- src_now: float32 [32, 64, 128], P('wide', 'shots'), parts along dimension 1, may hold values from -6 to 6
- src_old: float32 [32, 64, 128], P('wide', 'shots'), parts along dimension 1, may hold values from -6 to 6
- rcv_now: float32 [32, 256, 32], P('wide', 'shots'), parts along dimension 1, may hold values from -6 to 6
- rcv_old: float32 [32, 256, 32], P('wide', 'shots'), parts along dimension 1, may hold values from -6 to 6
- medium: float32 [3, 32, 128, 32], P(None, 'wide'), may hold values from 0.04 to 0.24
- wavelet: float32 [4], replicated, may hold values from -4 to 4
- shot: int32 [6], P('shots'), parts along dimension 0, may hold values from 0 to 31
- traces: float32 [32, 128, 4], P('wide', 'shots'), parts along dimension 1, may hold values from -6 to 6
- rec_x: int32 [32, 128], P('wide', 'shots'), parts along dimension 1, may hold values from 0 to 31
- lag_order: int32 [33], replicated, may hold values from 0 to 32, each once
Outputs:
- src_next: float32 [32, 64, 128], P('wide', 'shots'), parts along dimension 1
- src_prior: float32 [32, 64, 128], P('wide', 'shots'), parts along dimension 1
- rcv_next: float32 [32, 256, 32], P('wide', 'shots'), parts along dimension 1
- rcv_prior: float32 [32, 256, 32], P('wide', 'shots'), parts along dimension 1
- image: float32 [66, 32, 128, 32], P('shots', 'wide'), parts along dimension 0
The draws below stay inside these ranges and needn't reach their ends.
There are 2 independent parts, one for each index of `shots`. The reference program is written for one: setup_inputs(seed, part) draws one part's arguments, and reference() takes and returns one part's arrays. A program takes and returns all parts, laid end to end along the dimension named above; an argument that names none is the same for every part. Nothing has to cross between parts.
Inputs may be any that keep to these rules, and one draw needn't show every extreme that they name: `lag_order`: each of the 33 lag slots once.
All inputs are finite; a program needn't handle non-finite values.
Results may differ from the reference program's by a relative error of at most 0.0003.
Values sent between devices are 32-bit elements; how exact they have to be, the bound alone decides.
A program may use at most 64 MiB of HBM per device.

```python
import math
import jax
import jax.numpy as jnp
from jax import lax

Z = 128
RX = 64
STEPS = 4
LAGS = 33
X = 32
Y = 32


def place_ends(values, key, smallest, high):
    extent = values.shape
    spot = [jax.random.randint(jax.random.fold_in(key, axis), (), 0, extent[axis]) for axis in range(len(extent))]
    values = values.at[tuple(spot)].set(smallest)
    longest = extent.index(max(extent))
    spot[longest] = (spot[longest] + 1) % extent[longest]
    return values.at[tuple(spot)].set(high)


def shard_levels(own_key, extent, cuts, low, high):
    def one(axis_at, shards_of):
        steps = jax.random.uniform(jax.random.fold_in(jax.random.fold_in(own_key, 6), axis_at), (shards_of,), jnp.float32, low / len(cuts), high / len(cuts))
        return jnp.repeat(jnp.exp(steps), extent[axis_at] // shards_of).reshape((-1,) + (1,) * (len(extent) - axis_at - 1))

    gain = one(*cuts[0])
    for cut in cuts[1:]:
        gain = gain * one(*cut)
    return gain


def normal_values(key, extent, scale, reach, split=(), kind=jnp.bfloat16):
    entries = scale * jax.random.normal(key, extent, jnp.float32)
    if split:
        entries = entries * shard_levels(key, extent, split, -0.22, 0.18)
    return jnp.clip(entries, -reach, reach).astype(kind)


def setup_inputs(seed: int = 0, part: int = 0) -> dict:
    key_of = jax.random.split(jax.random.key(seed), 11)
    part_keys = jax.random.split(jax.random.fold_in(key_of[10], part), 11)
    return {
        "src_now": normal_values(part_keys[0], (X, Y, Z), 1.0, 6.0, ((0, 16),), jnp.float32),
        "src_old": normal_values(part_keys[1], (X, Y, Z), 1.0, 6.0, ((0, 16),), jnp.float32),
        "rcv_now": normal_values(part_keys[2], (Y, Z, X), 1.0, 6.0, ((0, 16),), jnp.float32),
        "rcv_old": normal_values(part_keys[3], (Y, Z, X), 1.0, 6.0, ((0, 16),), jnp.float32),
        "medium": jnp.clip(jnp.exp(math.log(0.24) - 1.7917595 * jax.random.uniform(key_of[4], (3, Y, Z, X), jnp.float32) ** shard_levels(key_of[4], (3, Y, Z, X), ((1, 16),), -0.2, 0.2)), 0.04, 0.24),
        "wavelet": normal_values(key_of[5], (STEPS,), 1.0, 4.0, (), jnp.float32),
        "shot": jax.random.randint(part_keys[6], (3,), 0, min(X, Y, Z)).astype(jnp.int32),
        "traces": normal_values(part_keys[7], (Y, RX, STEPS), 1.0, 6.0, ((0, 16),), jnp.float32),
        "rec_x": place_ends(jax.random.randint(part_keys[8], (Y, RX), 0, X), jax.random.fold_in(part_keys[8], 1), 0, X - 1).astype(jnp.int32),
        "lag_order": jax.random.permutation(key_of[9], LAGS).astype(jnp.int32),
    }


def window_sum(padded, dim, count):
    def window_at(start):
        return lax.slice_in_dim(padded, start, start + count, axis=dim)
    return (-1.0 / 12.0) * (window_at(0) + window_at(4)) + (4.0 / 3.0) * (window_at(1) + window_at(3)) - 2.5 * window_at(2)


def widen(field, dim):
    widths = [(0, 0)] * field.ndim
    widths[dim] = (2, 2)
    return jnp.pad(field, widths)


def second(field, dim):
    return window_sum(widen(field, dim), dim, field.shape[dim])


def lagged(snaps, lag_order):
    half = (lag_order.shape[0] - 1) // 2
    cells_x = snaps[0][0].shape[2]
    widths = ((0, 0), (0, 0), (half, half))
    padded = [(jnp.pad(source, widths), jnp.pad(receiver, widths)) for source, receiver in snaps]

    def one_plane(slot):
        offset = slot.astype(jnp.int32) - half
        total = None
        for source, receiver in padded:
            moved_src = lax.dynamic_slice_in_dim(source, (half - offset).astype(jnp.int32), cells_x, 2)
            moved_rcv = lax.dynamic_slice_in_dim(receiver, (half + offset).astype(jnp.int32), cells_x, 2)
            product = moved_src * moved_rcv
            total = product if total is None else total + product
        return total

    return lax.map(one_plane, lag_order)


def reference(src_now, src_old, rcv_now, rcv_old, medium, wavelet, shot, traces, rec_x, lag_order):
    cells_x, cells_y, cells_z = src_now.shape
    src_speed = jnp.transpose(medium, (0, 3, 1, 2))
    shot_cell = ((jnp.arange(cells_x, dtype=jnp.int32) == shot[0]).astype(jnp.float32)[:, None, None]
                 * (jnp.arange(cells_y, dtype=jnp.int32) == shot[1]).astype(jnp.float32)[None, :, None]
                 * (jnp.arange(cells_z, dtype=jnp.int32) == shot[2]).astype(jnp.float32)[None, None, :])
    onehot = (rec_x[:, :, None] == jnp.arange(cells_x, dtype=jnp.int32)[None, None, :]).astype(jnp.float32)
    snaps = []
    for step in range(wavelet.shape[0]):
        spread = src_speed[0] * second(src_now, 0) + src_speed[1] * second(src_now, 1) + src_speed[2] * second(src_now, 2)
        src_new = 2.0 * src_now - src_old + spread - wavelet[step] * shot_cell
        spread_rcv = medium[0] * second(rcv_now, 2) + medium[1] * second(rcv_now, 0) + medium[2] * second(rcv_now, 1)
        rcv_new = 2.0 * rcv_now - rcv_old + spread_rcv
        surface = jnp.einsum("yr,yrx->yx", traces[:, :, step], onehot, precision=lax.Precision.HIGHEST)
        rcv_new = rcv_new.at[:, 0, :].add(surface)
        src_old, src_now = src_now, src_new
        rcv_old, rcv_now = rcv_now, rcv_new
        if step % 2 == 1:
            snaps.append((jnp.transpose(src_now, (1, 2, 0)), rcv_now))
    image = lagged(snaps, lag_order)
    return src_now, src_old, rcv_now, rcv_old, image
```

```python
import functools
import math

import jax
import jax.numpy as jnp
from jax import lax
from jax.experimental import pallas as pl
from jax.experimental.pallas import tpu as pltpu
from jax.sharding import PartitionSpec as P

REACH = 2
EDGE = 8
OUTER, INNER, CENTRE = -1.0 / 12.0, 4.0 / 3.0, -2.5
RCV, SRC, ALT = 0, 1, 2
FIELDS = (RCV, SRC, ALT)
PARTS = 3
MESH = pl.DeviceIdType.MESH


def second(window):
    return (
        OUTER * (window(-2) + window(2)) + INNER * (window(-1) + window(1)) + CENTRE * window(0)
    )


def window_kernel(
    devices,
    src_now_in,
    src_old_in,
    rcv_now_in,
    rcv_old_in,
    medium_in,
    wavelet_in,
    shot_in,
    traces_in,
    rec_x_in,
    lag_order_in,
    src_next,
    src_prior,
    rcv_next,
    rcv_prior,
    board,
    src_old,
    rcv_old,
    medium,
    wavelet,
    shot,
    traces,
    rec_x,
    lag_order,
    padded,
    staged,
    landed,
    levels,
    partial,
    surface,
    spot,
    spot_alt,
    out_send,
    out_recv,
    halo_send,
    halo_recv,
    load_sems,
):
    me = lax.axis_index("wide")
    slab, cells, cells_z = src_old.shape
    steps = wavelet.shape[0]
    rows = 2 * PARTS * slab
    block = slab * rows
    inside = pl.ds(EDGE, cells)
    own_planes = pl.ds(REACH, slab)

    lags = lag_order.shape[0]
    half = (lags - 1) // 2
    middle = devices // 2
    far_first = sorted(range(1, devices), key=lambda distance: abs(distance - middle))

    loads = []
    for index, (source, target) in enumerate(
        (
            (src_now_in, levels.at[0, ALT, own_planes, inside]),
            (src_old_in, src_old),
            (medium_in, medium),
            (rcv_now_in, levels.at[0, RCV, own_planes, inside]),
            (shot_in, shot),
            (traces_in, traces),
            (rec_x_in, rec_x),
            (rcv_old_in, rcv_old),
            (wavelet_in, wavelet),
            (lag_order_in, lag_order),
        )
    ):
        loads.append(pltpu.make_async_copy(source, target, load_sems.at[index]))
    for load in loads[:3]:
        load.start()

    barrier = pltpu.get_barrier_semaphore()
    for distance in far_first:
        pl.semaphore_signal(
            barrier,
            inc=1,
            device_id={"wide": lax.rem(me + distance, devices)},
            device_id_type=MESH,
        )
    for load in loads[3:]:
        load.start()

    zero_edge = jnp.zeros((EDGE, cells_z), jnp.float32)
    zero_plane = jnp.zeros((cells, cells_z), jnp.float32)
    zero_half = jnp.zeros((half, cells_z), jnp.float32)
    for level in range(steps):
        for field in FIELDS:
            for at in range(REACH, REACH + slab):
                levels[level, field, at, 0:EDGE, :] = zero_edge
                levels[level, field, at, EDGE + cells : EDGE + cells + EDGE, :] = zero_edge

    row_at = lax.broadcasted_iota(jnp.int32, (cells, cells_z), 0)
    lane_at = lax.broadcasted_iota(jnp.int32, (cells, cells_z), 1)

    def along_rows(field, level, at):
        centre = levels[level, field, REACH + at, inside, :]

        def window(shift):
            if shift == 0:
                return centre
            return levels[level, field, REACH + at, pl.ds(EDGE + shift, cells), :]

        return second(window)

    for load in loads[:3]:
        load.wait()
    for at in range(slab):
        sent_rows = (
            lambda: levels[0, ALT, REACH + at, inside, :],
            lambda: src_old[at],
            lambda: along_rows(ALT, 0, at),
        )
        for part, rows_of in enumerate(sent_rows):
            partial[0, 0] = rows_of()
            for y in range(slab):
                into = at * rows + part * slab + y
                staged[pl.ds(into, devices, stride=block), :] = partial[
                    0, 0, pl.ds(y, devices, stride=slab), :
                ]
        for part in range(PARTS):
            for x in range(slab):
                into = at * rows + (PARTS + part) * slab + x
                staged[pl.ds(into, devices, stride=block), :] = medium[
                    part, at, pl.ds(x, devices, stride=slab), :
                ]

    pl.semaphore_wait(barrier, devices - 1)

    def out_copy(peer):
        return pltpu.make_async_remote_copy(
            src_ref=staged.at[pl.ds(pl.multiple_of(peer * block, 8), block)],
            dst_ref=landed.at[pl.ds(pl.multiple_of(me * block, 8), block)],
            send_sem=out_send,
            recv_sem=out_recv,
            device_id={"wide": peer},
            device_id_type=MESH,
        )

    def halo_copy(field, level, side):
        first = slab if side == 0 else REACH
        source = levels.at[level, field, pl.ds(first, REACH), inside]
        into = 0 if side == 0 else REACH + slab
        peer = me + 1 if side == 0 else me - 1
        return pltpu.make_async_remote_copy(
            src_ref=source,
            dst_ref=levels.at[level, field, pl.ds(into, REACH), inside],
            send_sem=halo_send.at[field, level, side],
            recv_sem=halo_recv.at[field, level, side],
            device_id={"wide": peer},
            device_id_type=MESH,
        )

    def each_side(act):
        @pl.when(me < devices - 1)
        def _():
            act(0)

        @pl.when(me > 0)
        def _():
            act(1)

    def send_halo(field, level):
        each_side(lambda side: halo_copy(field, level, side).start())

    def wait_halo(field, level):
        each_side(lambda side: halo_copy(field, level, 1 - side).wait_recv())

    def wait_sent(field, level):
        each_side(lambda side: halo_copy(field, level, side).wait_send())

    for distance in far_first:
        out_copy(lax.rem(me + distance, devices)).start()

    for load in loads[3:]:
        load.wait()
    send_halo(RCV, 0)
    send_halo(ALT, 0)

    own = pl.ds(pl.multiple_of(me * block, 8), block)
    landed[own, :] = staged[own, :]

    for snap in range(padded.shape[0]):
        for field in (RCV, SRC):
            for y in range(slab):
                padded[snap, field, y, 0:half, :] = zero_half
                padded[snap, field, y, half + cells : 2 * half + cells, :] = zero_half

    @pl.when(me == 0)
    def _():
        for level in range(steps):
            for field in FIELDS:
                for at in range(REACH):
                    levels[level, field, at, inside, :] = zero_plane

    @pl.when(me == devices - 1)
    def _():
        for level in range(steps):
            for field in FIELDS:
                for at in range(REACH):
                    levels[level, field, REACH + slab + at, inside, :] = zero_plane

    deep = lane_at == shot[2]
    column = ((row_at == shot[0]) & deep).astype(jnp.float32)
    column_alt = ((row_at == shot[1]) & deep).astype(jnp.float32)
    for at in range(slab):
        spot[at] = column * (me * slab + at == shot[1]).astype(jnp.float32)
        spot_alt[at] = column_alt * (me * slab + at == shot[0]).astype(jnp.float32)
    x_at = lax.broadcasted_iota(jnp.int32, (cells, traces.shape[2]), 0)
    for y in range(slab):
        onehot = (x_at == rec_x[y : y + 1, :]).astype(jnp.float32)
        for step in range(steps):
            total = jnp.sum(onehot * traces[y, step : step + 1, :], axis=1, keepdims=True)
            surface[step, y] = jnp.where(lane_at == 0, total, 0.0)

    def arrived_rows(part, at):
        return landed[pl.ds(part * slab + at, cells, stride=rows), :]

    def older(field, level, at):
        if level > 0:
            return levels[level - 1, field, REACH + at, inside, :]
        if field == RCV:
            return rcv_old[at]
        if field == ALT:
            return src_old[at]
        return arrived_rows(1, at)

    def speeds(field, at):
        if field == ALT:
            return tuple(arrived_rows(PARTS + part, at) for part in (0, 1, 2))
        return tuple(medium[part, at] for part in (1, 0, 2))

    def local(field, level):
        for at in range(slab):
            centre = levels[level, field, REACH + at, inside, :]
            _, rows_speed, lanes_speed = speeds(field, at)

            def along_lanes(shift):
                if shift == 0:
                    return centre
                turned = pltpu.roll(centre, (-shift) % cells_z, 1)
                kept = lane_at >= -shift if shift < 0 else lane_at < cells_z - shift
                return jnp.where(kept, turned, 0.0)

            partial[field, at] = (
                2.0 * centre
                - older(field, level, at)
                + rows_speed * along_rows(field, level, at)
                + lanes_speed * second(along_lanes)
            )

    def finish(field, level):
        for at in range(slab):
            def along_planes(shift):
                return levels[level, field, REACH + at + shift, inside, :]

            if field == SRC and level == 0:
                bend = arrived_rows(2, at)
            else:
                bend = second(along_planes)
            if field == RCV:
                added = surface[level, at]
            else:
                added = -wavelet[level] * (spot if field == SRC else spot_alt)[at]
            levels[level + 1, field, REACH + at, inside, :] = (
                partial[field, at] + speeds(field, at)[0] * bend + added
            )

    def keep(field, level):
        snap = level // 2 - 1
        for y in range(slab):
            padded[snap, field, y, half : half + cells, :] = levels[
                level, field, REACH + y, inside, :
            ]

    def correlate(snap):
        for plane in range(lags):
            slot = lag_order[plane]
            at_src = pl.ds(2 * half - slot, cells)
            at_rcv = pl.ds(slot, cells)
            for y in range(slab):
                product = padded[snap, SRC, y, at_src, :] * padded[snap, RCV, y, at_rcv, :]
                board[plane, y] = product if snap == 0 else board[plane, y] + product

    local(RCV, 0)
    wait_halo(RCV, 0)
    finish(RCV, 0)
    send_halo(RCV, 1)
    local(RCV, 1)
    wait_halo(ALT, 0)

    arrived = landed.at[pl.ds(0, (devices - 1) * block)]
    pltpu.make_async_copy(arrived, arrived, out_recv).wait()
    for y in range(slab):
        levels[0, SRC, REACH + y, inside, :] = arrived_rows(0, y)
    for field in (ALT, SRC):
        local(field, 0)
        finish(field, 0)
        send_halo(field, 1)
    for level in range(1, steps):
        local(ALT, level)
        local(SRC, level)
        if level == steps - 1:
            keep(SRC, 2)
            keep(RCV, 2)
            correlate(0)
        wait_halo(RCV, level)
        finish(RCV, level)
        if level + 1 < steps:
            send_halo(RCV, level + 1)
            local(RCV, level + 1)
        for field in (ALT, SRC):
            wait_halo(field, level)
            finish(field, level)
            if level + 1 < steps:
                send_halo(field, level + 1)

    keep(SRC, steps)
    keep(RCV, steps)
    correlate(1)
    for at in range(slab):
        src_next[at] = levels[steps, ALT, REACH + at, inside, :]
        src_prior[at] = levels[steps - 1, ALT, REACH + at, inside, :]
        rcv_next[at] = levels[steps, RCV, REACH + at, inside, :]
        rcv_prior[at] = levels[steps - 1, RCV, REACH + at, inside, :]

    sent = staged.at[pl.ds(0, (devices - 1) * block)]
    pltpu.make_async_copy(sent, sent, out_send).wait()
    for level in range(steps):
        for field in FIELDS:
            if level > 0 or field != SRC:
                wait_sent(field, level)


def deliver_kernel(*refs):
    count = (len(refs) - 1) // 2
    copies = [
        pltpu.make_async_copy(refs[i], refs[count + i], refs[-1].at[i]) for i in range(count)
    ]
    for copy in copies:
        copy.start()
    for copy in copies:
        copy.wait()


def solution(mesh):
    devices = mesh.shape["wide"]

    def on_device(
        src_now, src_old, rcv_now, rcv_old, medium, wavelet, shot, traces, rec_x, lag_order
    ):
        slab, cells, cells_z = src_now.shape
        assert rcv_now.shape == (slab, cells_z, cells) and slab >= REACH
        assert slab * devices == cells
        steps = wavelet.shape[0]
        lags = lag_order.shape[0]
        half = (lags - 1) // 2
        span = slab + 2 * REACH
        rows = 2 * PARTS * slab
        f32 = jnp.float32
        vmem = pl.BlockSpec(memory_space=pltpu.VMEM)
        hbm = pl.BlockSpec(memory_space=pltpu.HBM)
        field_shape = jax.ShapeDtypeStruct((slab, cells, cells_z), f32)
        board_shape = jax.ShapeDtypeStruct((lags, slab, cells, cells_z), f32)
        shapes = (field_shape,) * 4 + (board_shape,)
        taken = steps // 2
        turn = lambda array: jnp.swapaxes(array, -1, -2)
        like = lambda array: pltpu.VMEM(array.shape, array.dtype)
        scalars = lambda array: pltpu.SMEM(array.shape, array.dtype)
        rcv_now, rcv_old, medium, traces = map(turn, (rcv_now, rcv_old, medium, traces))
        scratch = [
            like(src_old),
            like(rcv_old),
            like(medium),
            scalars(wavelet),
            scalars(shot),
            like(traces),
            like(rec_x),
            scalars(lag_order),
            pltpu.VMEM((taken, 2, slab, cells + 2 * half, cells_z), f32),
            pltpu.VMEM((cells * rows, cells_z), f32),
            pltpu.VMEM((cells * rows, cells_z), f32),
            pltpu.VMEM((steps + 1, 3, span, cells + 2 * EDGE, cells_z), f32),
            pltpu.VMEM((3, slab, cells, cells_z), f32),
            pltpu.VMEM((steps, slab, cells, cells_z), f32),
            pltpu.VMEM((slab, cells, cells_z), f32),
            pltpu.VMEM((slab, cells, cells_z), f32),
        ]
        held = sum(4 * math.prod(each.shape) for each in scratch + list(shapes))
        results = pl.pallas_call(
            functools.partial(window_kernel, devices),
            out_shape=shapes,
            in_specs=[hbm] * 10,
            out_specs=(vmem,) * 5,
            scratch_shapes=scratch
            + [pltpu.SemaphoreType.DMA] * 2
            + [
                pltpu.SemaphoreType.DMA((3, steps, 2)),
                pltpu.SemaphoreType.DMA((3, steps, 2)),
                pltpu.SemaphoreType.DMA((10,)),
            ],
            compiler_params=pltpu.CompilerParams(
                collective_id=0, has_side_effects=True, vmem_limit_bytes=held + (4 << 20)
            ),
            name="window",
        )(
            *(
                pltpu.with_memory_space_constraint(array, pltpu.HBM)
                for array in (
                    src_now,
                    src_old,
                    rcv_now,
                    rcv_old,
                    medium,
                    wavelet,
                    shot,
                    traces,
                    rec_x,
                    lag_order,
                )
            )
        )
        outs = pl.pallas_call(
            deliver_kernel,
            out_shape=shapes,
            in_specs=[vmem] * 5,
            out_specs=(hbm,) * 5,
            scratch_shapes=[pltpu.SemaphoreType.DMA((5,))],
            compiler_params=pltpu.CompilerParams(vmem_limit_bytes=held + (4 << 20)),
            name="deliver",
        )(*results)
        return outs[0], outs[1], turn(outs[2]), turn(outs[3]), turn(outs[4])

    return jax.shard_map(
        on_device,
        mesh=mesh,
        in_specs=(
            P("wide", "shots", None),
            P("wide", "shots", None),
            P("wide", "shots", None),
            P("wide", "shots", None),
            P(None, "wide", None, None),
            P(),
            P("shots"),
            P("wide", "shots", None),
            P("wide", "shots"),
            P(),
        ),
        out_specs=(
            P("wide", "shots", None),
            P("wide", "shots", None),
            P("wide", "shots", None),
            P("wide", "shots", None),
            P("shots", "wide", None, None),
        ),
        check_vma=False,
    )
```

```python
import functools
import math

import jax
import jax.numpy as jnp
from jax import lax
from jax.experimental import pallas as pl
from jax.experimental.pallas import tpu as pltpu
from jax.sharding import PartitionSpec as P

REACH = 2
EDGE = 8
OUTER, INNER, CENTRE = -1.0 / 12.0, 4.0 / 3.0, -2.5
SRC, ALT = 0, 1
FIELDS = (SRC, ALT)
PARTS = 3
LEFT, RIGHT = 0, 1
MESH = pl.DeviceIdType.MESH


def second(window):
    return (
        OUTER * (window(-2) + window(2)) + INNER * (window(-1) + window(1)) + CENTRE * window(0)
    )


def window_kernel(
    devices,
    src_now_in,
    src_old_in,
    rcv_now_in,
    rcv_old_in,
    medium_in,
    wavelet_in,
    shot_in,
    traces_in,
    rec_x_in,
    lag_order_in,
    src_next,
    src_prior,
    rcv_next,
    rcv_prior,
    board,
    src_old,
    rcv_old,
    medium,
    medium_alt,
    wavelet,
    shot,
    traces,
    rec_x,
    lag_order,
    padded,
    staged,
    landed,
    waves,
    echoes,
    partial,
    partial_rcv,
    surface,
    columns,
    out_send,
    out_recv,
    halo_send,
    halo_recv,
    echo_send,
    echo_recv,
    pair_send,
    pair_recv,
    load_sems,
):
    me = lax.axis_index("wide")
    pairs = devices // 2
    pair = me // 2
    odd = lax.rem(me, 2)
    slab, cells, cells_z = rcv_old.shape
    both = 2 * slab
    steps = wavelet.shape[0]
    last = steps - 1
    rows = 2 * PARTS * both
    block = slab * rows
    inside = pl.ds(EDGE, cells)
    mine = pl.ds(odd * slab, slab)
    mine_waves = pl.ds(REACH + odd * slab, slab)
    own_echoes = pl.ds(REACH, slab)

    lags = lag_order.shape[0]
    half = (lags - 1) // 2
    far_first = sorted(range(1, devices), key=lambda distance: abs(distance - devices // 2))
    far_pairs = sorted(range(1, pairs), key=lambda distance: abs(distance - pairs // 2))

    def when_first(act):
        pl.when(odd == 0)(act)

    def when_second(act):
        pl.when(odd == 1)(act)

    loads = []
    for index, (source, target) in enumerate(
        (
            (src_now_in, waves.at[0, ALT, mine_waves, inside]),
            (src_old_in, src_old.at[mine]),
            (medium_in, medium.at[:, mine]),
            (rcv_now_in, echoes.at[0, own_echoes, inside]),
            (shot_in, shot),
            (traces_in, traces),
            (rec_x_in, rec_x),
            (rcv_old_in, rcv_old),
            (wavelet_in, wavelet),
            (lag_order_in, lag_order),
        )
    ):
        loads.append(pltpu.make_async_copy(source, target, load_sems.at[index]))
    for load in loads[:3]:
        load.start()

    barrier = pltpu.get_barrier_semaphore()

    def greet(peer):
        pl.semaphore_signal(
            barrier, inc=1, device_id={"wide": peer}, device_id_type=MESH
        )

    @when_second
    def _():
        for distance in far_first:
            greet(lax.rem(me + distance, devices))

    @when_first
    def _():
        greet(me + 1)
        pl.when(pair > 0)(lambda: greet(me - 1))

    for load in loads[3:]:
        load.start()

    zero_edge = jnp.zeros((EDGE, cells_z), jnp.float32)
    zero_plane = jnp.zeros((cells, cells_z), jnp.float32)
    zero_half = jnp.zeros((half, cells_z), jnp.float32)

    for field in FIELDS:
        for level in range(steps):
            for at in range(REACH, REACH + both):
                waves[level, field, at, 0:EDGE, :] = zero_edge
                waves[level, field, at, EDGE + cells : EDGE + cells + EDGE, :] = zero_edge
    for level in range(steps):
        for at in range(REACH, REACH + slab):
            echoes[level, at, 0:EDGE, :] = zero_edge
            echoes[level, at, EDGE + cells : EDGE + cells + EDGE, :] = zero_edge

    row_at = lax.broadcasted_iota(jnp.int32, (cells, cells_z), 0)
    lane_at = lax.broadcasted_iota(jnp.int32, (cells, cells_z), 1)

    def along_rows(plane):
        def window(shift):
            return plane(pl.ds(EDGE + shift, cells))

        return second(window)

    for load in loads[:3]:
        load.wait()
    for at in range(slab):
        def now_rows(where):
            return waves[0, ALT, REACH + odd * slab + at, where, :]

        sent_rows = (
            lambda: now_rows(inside),
            lambda: src_old[odd * slab + at],
            lambda: along_rows(now_rows),
        )
        for part, rows_of in enumerate(sent_rows):
            partial[part, at] = rows_of()
            for y in range(both):
                into = at * rows + part * both + y
                staged[pl.ds(into, pairs, stride=block), :] = partial[
                    part, at, pl.ds(y, pairs, stride=both), :
                ]
        for part in range(PARTS):
            for x in range(both):
                into = at * rows + (PARTS + part) * both + x
                staged[pl.ds(into, pairs, stride=block), :] = medium[
                    part, odd * slab + at, pl.ds(x, pairs, stride=both), :
                ]

    pl.semaphore_wait(barrier, pairs + odd * (pair < pairs - 1).astype(jnp.int32))

    def remote(source, target, send, recv, peer):
        return pltpu.make_async_remote_copy(
            src_ref=source,
            dst_ref=target,
            send_sem=send,
            recv_sem=recv,
            device_id={"wide": peer},
            device_id_type=MESH,
        )

    def out_copy(to):
        return remote(
            staged.at[pl.ds(pl.multiple_of(to * block, 8), block)],
            landed.at[pl.ds(pl.multiple_of(me * block, 8), block)],
            out_send,
            out_recv,
            2 * to + 1,
        )

    def pair_copy(index):
        early = index < 3
        source = (
            waves.at[0, ALT, pl.ds(REACH, slab), inside],
            src_old.at[pl.ds(0, slab)],
            medium.at[:, pl.ds(0, slab)],
            medium_alt.at[:, pl.ds(0, slab)],
            waves.at[last - 1, :, pl.ds(REACH, slab), inside],
            waves.at[last, :, pl.ds(REACH, both), inside],
        )[index]
        peer = 2 * pair + 1 if early else 2 * pair
        return remote(source, source, pair_send.at[index], pair_recv.at[index], peer)

    def halo_copy(field, level, side):
        first = both if side == LEFT else REACH
        into = 0 if side == LEFT else REACH + both
        to = pair + 1 if side == LEFT else pair - 1
        peer = 2 * to if level == last and side == LEFT else 2 * to + 1
        return remote(
            waves.at[level, field, pl.ds(first, REACH), inside],
            waves.at[level, field, pl.ds(into, REACH), inside],
            halo_send.at[field, level, side],
            halo_recv.at[field, level, side],
            peer,
        )

    def sends_to(side):
        return pair < pairs - 1 if side == LEFT else pair > 0

    def gets_from(side):
        return pair > 0 if side == LEFT else pair < pairs - 1

    def send_halo(field, level, side):
        pl.when(sends_to(side))(lambda: halo_copy(field, level, side).start())

    def wait_sent(field, level, side):
        pl.when(sends_to(side))(lambda: halo_copy(field, level, side).wait_send())

    def wait_halo(field, level, side):
        pl.when(gets_from(side))(lambda: halo_copy(field, level, side).wait_recv())

    def echo_copy(level, side):
        first = slab if side == LEFT else REACH
        into = 0 if side == LEFT else REACH + slab
        return remote(
            echoes.at[level, pl.ds(first, REACH), inside],
            echoes.at[level, pl.ds(into, REACH), inside],
            echo_send.at[level, side],
            echo_recv.at[level, side],
            me + 1 if side == LEFT else me - 1,
        )

    def each_side(act):
        pl.when(me < devices - 1)(lambda: act(LEFT))
        pl.when(me > 0)(lambda: act(RIGHT))

    def send_echo(level):
        each_side(lambda side: echo_copy(level, side).start())

    def wait_echo(level):
        each_side(lambda side: echo_copy(level, 1 - side).wait_recv())

    loads[3].wait()
    send_echo(0)

    for distance in far_pairs:
        out_copy(lax.rem(pair + distance, pairs)).start()

    for load in loads[4:]:
        load.wait()

    @when_first
    def _():
        out_copy(pair).start()
        send_halo(ALT, 0, RIGHT)
        for index in range(3):
            pair_copy(index).start()

    @when_second
    def _():
        send_halo(ALT, 0, LEFT)
        own = pl.ds(pl.multiple_of(me * block, 8), block)
        landed[own, :] = staged[pl.ds(pl.multiple_of(pair * block, 8), block), :]


    for snap in range(padded.shape[0]):
        for field in range(2):
            for y in range(slab):
                padded[snap, field, y, 0:half, :] = zero_half
                padded[snap, field, y, half + cells : 2 * half + cells, :] = zero_half

    def clear_planes(first):
        for level in range(steps):
            for field in FIELDS:
                for at in range(REACH):
                    waves[level, field, first + at, inside, :] = zero_plane

    pl.when(pair == 0)(lambda: clear_planes(0))
    pl.when(pair == pairs - 1)(lambda: clear_planes(REACH + both))

    def clear_echoes(first):
        for level in range(steps):
            for at in range(REACH):
                echoes[level, first + at, inside, :] = zero_plane

    pl.when(me == 0)(lambda: clear_echoes(0))
    pl.when(me == devices - 1)(lambda: clear_echoes(REACH + slab))

    deep = lane_at == shot[2]
    columns[SRC] = ((row_at == shot[0]) & deep).astype(jnp.float32)
    columns[ALT] = ((row_at == shot[1]) & deep).astype(jnp.float32)
    x_at = lax.broadcasted_iota(jnp.int32, (cells, traces.shape[2]), 0)
    for y in range(slab):
        onehot = (x_at == rec_x[y : y + 1, :]).astype(jnp.float32)
        for step in range(steps):
            total = jnp.sum(onehot * traces[y, step : step + 1, :], axis=1, keepdims=True)
            surface[step, y] = jnp.where(lane_at == 0, total, 0.0)

    def arrived_rows(part, at):
        return landed[pl.ds(part * both + at, cells, stride=rows), :]

    def along_lanes(centre):
        def window(shift):
            if shift == 0:
                return centre
            turned = pltpu.roll(centre, (-shift) % cells_z, 1)
            kept = lane_at >= -shift if shift < 0 else lane_at < cells_z - shift
            return jnp.where(kept, turned, 0.0)

        return second(window)

    def flat(plane, older, rows_speed, lanes_speed):
        centre = plane(inside)
        return (
            2.0 * centre
            - older
            + rows_speed * along_rows(plane)
            + lanes_speed * along_lanes(centre)
        )

    def speed(field, part, at):
        if field == ALT:
            return medium_alt[part, at]
        return medium[(1, 0, 2)[part], at]

    def local(field, level, ats):
        for at in ats:
            def plane(where):
                return waves[level, field, REACH + at, where, :]

            if level > 0:
                older = waves[level - 1, field, REACH + at, inside, :]
            elif field == ALT:
                older = src_old[at]
            else:
                older = arrived_rows(1, at)
            partial[field, at] = flat(plane, older, speed(field, 1, at), speed(field, 2, at))

    def finish(field, level, ats):
        for at in ats:
            def along_planes(shift):
                return waves[level, field, REACH + at + shift, inside, :]

            if field == SRC and level == 0:
                bend = arrived_rows(2, at)
            else:
                bend = second(along_planes)
            hit = (pair * both + at == shot[1 if field == SRC else 0]).astype(jnp.float32)
            waves[level + 1, field, REACH + at, inside, :] = (
                partial[field, at]
                + speed(field, 0, at) * bend
                - (wavelet[level] * hit) * columns[field]
            )

    def local_both(level, ats):
        for field in FIELDS:
            local(field, level, ats)

    def local_rcv(level):
        for at in range(slab):
            def plane(where):
                return echoes[level, REACH + at, where, :]

            older = echoes[level - 1, REACH + at, inside, :] if level > 0 else rcv_old[at]
            here = odd * slab + at
            partial_rcv[at] = flat(plane, older, medium[0, here], medium[2, here])

    def finish_rcv(level):
        for at in range(slab):
            def along_planes(shift):
                return echoes[level, REACH + at + shift, inside, :]

            echoes[level + 1, REACH + at, inside, :] = (
                partial_rcv[at]
                + medium[1, odd * slab + at] * second(along_planes)
                + surface[level, at]
            )

    def keep_src(level):
        for y in range(slab):
            padded[level // 2 - 1, 0, y, half : half + cells, :] = waves[
                level, SRC, REACH + odd * slab + y, inside, :
            ]

    def keep_rcv(level):
        for y in range(slab):
            padded[level // 2 - 1, 1, y, half : half + cells, :] = echoes[
                level, REACH + y, inside, :
            ]

    def correlate(snap):
        for plane in range(lags):
            slot = lag_order[plane]
            at_src = pl.ds(2 * half - slot, cells)
            at_rcv = pl.ds(slot, cells)
            for y in range(slab):
                product = padded[snap, 0, y, at_src, :] * padded[snap, 1, y, at_rcv, :]
                board[plane, y] = product if snap == 0 else board[plane, y] + product

    everyone = range(both)
    firsts, seconds = range(slab), range(slab, both)

    def advance_rcv(level):
        wait_echo(level)
        finish_rcv(level)
        if level < last:
            send_echo(level + 1)
            local_rcv(level + 1)

    local_rcv(0)
    advance_rcv(0)

    @when_second
    def _():
        for index in range(3):
            pair_copy(index).wait_recv()
        for side in (LEFT, RIGHT):
            wait_halo(ALT, 0, side)
        arrived = landed.at[pl.ds(0, (devices - 1) * block)]
        pltpu.make_async_copy(arrived, arrived, out_recv).wait()
        for at in everyone:
            waves[0, SRC, REACH + at, inside, :] = arrived_rows(0, at)
        for field in FIELDS:
            if field == ALT:
                for at in everyone:
                    for part in range(PARTS):
                        medium_alt[part, at] = arrived_rows(PARTS + part, at)
            local(field, 0, everyone)
            finish(field, 0, everyone)
            for side in (RIGHT, LEFT):
                send_halo(field, 1, side)
        pair_copy(3).start()
        local_both(1, everyone)
        for field in FIELDS:
            for side in (LEFT, RIGHT):
                wait_sent(field, 1, side)

    advance_rcv(1)
    for level in range(1, last):

        @when_second
        def _():
            for field in FIELDS:
                for side in (LEFT, RIGHT):
                    wait_halo(field, level, side)
                finish(field, level, everyone)
                for side in (RIGHT, LEFT):
                    send_halo(field, level + 1, side)
            if level + 1 == last - 1:
                pair_copy(4).start()
            if level + 1 == last:
                pair_copy(5).start()
            local_both(level + 1, everyone if level + 1 < last else seconds)
            for field in FIELDS:
                for side in (LEFT, RIGHT):
                    wait_sent(field, level + 1, side)

        advance_rcv(level + 1)

    @when_first
    def _():
        for index in (3, 4):
            pair_copy(index).wait_recv()

    keep_src(2)
    keep_rcv(2)
    keep_rcv(steps)
    correlate(0)
    for at in range(slab):
        rcv_next[at] = echoes[steps, REACH + at, inside, :]
        rcv_prior[at] = echoes[last, REACH + at, inside, :]

    @when_first
    def _():
        pair_copy(5).wait_recv()
        local_both(last, firsts)

    def arrive(field):
        @when_second
        def _():
            wait_halo(field, last, RIGHT)
            finish(field, last, seconds)

        @when_first
        def _():
            wait_halo(field, last, LEFT)
            finish(field, last, firsts)

    arrive(SRC)
    keep_src(steps)
    correlate(1)
    arrive(ALT)
    for at in range(slab):
        src_next[at] = waves[steps, ALT, REACH + odd * slab + at, inside, :]
        src_prior[at] = waves[last, ALT, REACH + odd * slab + at, inside, :]

    @when_first
    def _():
        sent = staged.at[pl.ds(0, pairs * block)]
        pltpu.make_async_copy(sent, sent, out_send).wait()
        wait_sent(ALT, 0, RIGHT)
        for index in range(3):
            pair_copy(index).wait_send()

    @when_second
    def _():
        sent = staged.at[pl.ds(0, (pairs - 1) * block)]
        pltpu.make_async_copy(sent, sent, out_send).wait()
        wait_sent(ALT, 0, LEFT)
        for index in range(3, 6):
            pair_copy(index).wait_send()

    for level in range(steps):
        each_side(lambda side: echo_copy(level, side).wait_send())


def deliver_kernel(*refs):
    count = (len(refs) - 1) // 2
    copies = [
        pltpu.make_async_copy(refs[i], refs[count + i], refs[-1].at[i]) for i in range(count)
    ]
    for copy in copies:
        copy.start()
    for copy in copies:
        copy.wait()


def solution(mesh):
    devices = mesh.shape["wide"]

    def on_device(
        src_now, src_old, rcv_now, rcv_old, medium, wavelet, shot, traces, rec_x, lag_order
    ):
        slab, cells, cells_z = src_now.shape
        assert rcv_now.shape == (slab, cells_z, cells) and slab >= REACH
        assert slab * devices == cells and devices % 2 == 0
        steps = wavelet.shape[0]
        lags = lag_order.shape[0]
        half = (lags - 1) // 2
        rows = 4 * PARTS * slab
        f32 = jnp.float32
        vmem = pl.BlockSpec(memory_space=pltpu.VMEM)
        hbm = pl.BlockSpec(memory_space=pltpu.HBM)
        field_shape = jax.ShapeDtypeStruct((slab, cells, cells_z), f32)
        board_shape = jax.ShapeDtypeStruct((lags, slab, cells, cells_z), f32)
        shapes = (field_shape,) * 4 + (board_shape,)
        taken = steps // 2
        turn = lambda array: jnp.swapaxes(array, -1, -2)
        like = lambda array: pltpu.VMEM(array.shape, array.dtype)
        scalars = lambda array: pltpu.SMEM(array.shape, array.dtype)
        rcv_now, rcv_old, medium, traces = map(turn, (rcv_now, rcv_old, medium, traces))
        both = 2 * slab
        field = lambda *lead: pltpu.VMEM((*lead, cells, cells_z), f32)
        wide = lambda *lead: pltpu.VMEM((*lead, cells + 2 * EDGE, cells_z), f32)
        scratch = [
            field(both),
            like(rcv_old),
            field(PARTS, both),
            field(PARTS, both),
            scalars(wavelet),
            scalars(shot),
            like(traces),
            like(rec_x),
            scalars(lag_order),
            pltpu.VMEM((taken, 2, slab, cells + 2 * half, cells_z), f32),
            pltpu.VMEM((devices // 2 * slab * rows, cells_z), f32),
            pltpu.VMEM((devices * slab * rows, cells_z), f32),
            wide(steps + 1, 2, both + 2 * REACH),
            wide(steps + 1, slab + 2 * REACH),
            field(PARTS, both),
            field(slab),
            field(steps, slab),
            field(2),
        ]
        held = sum(4 * math.prod(each.shape) for each in scratch + list(shapes))
        results = pl.pallas_call(
            functools.partial(window_kernel, devices),
            out_shape=shapes,
            in_specs=[hbm] * 10,
            out_specs=(vmem,) * 5,
            scratch_shapes=scratch
            + [pltpu.SemaphoreType.DMA] * 2
            + [pltpu.SemaphoreType.DMA((2, steps, 2))] * 2
            + [pltpu.SemaphoreType.DMA((steps, 2))] * 2
            + [pltpu.SemaphoreType.DMA((6,))] * 2
            + [pltpu.SemaphoreType.DMA((10,))],
            compiler_params=pltpu.CompilerParams(
                collective_id=0, has_side_effects=True, vmem_limit_bytes=held + (4 << 20)
            ),
            name="window",
        )(
            *(
                pltpu.with_memory_space_constraint(array, pltpu.HBM)
                for array in (
                    src_now,
                    src_old,
                    rcv_now,
                    rcv_old,
                    medium,
                    wavelet,
                    shot,
                    traces,
                    rec_x,
                    lag_order,
                )
            )
        )
        outs = pl.pallas_call(
            deliver_kernel,
            out_shape=shapes,
            in_specs=[vmem] * 5,
            out_specs=(hbm,) * 5,
            scratch_shapes=[pltpu.SemaphoreType.DMA((5,))],
            compiler_params=pltpu.CompilerParams(vmem_limit_bytes=held + (4 << 20)),
            name="deliver",
        )(*results)
        return outs[0], outs[1], turn(outs[2]), turn(outs[3]), turn(outs[4])

    return jax.shard_map(
        on_device,
        mesh=mesh,
        in_specs=(
            P("wide", "shots", None),
            P("wide", "shots", None),
            P("wide", "shots", None),
            P("wide", "shots", None),
            P(None, "wide", None, None),
            P(),
            P("shots"),
            P("wide", "shots", None),
            P("wide", "shots"),
            P(),
        ),
        out_specs=(
            P("wide", "shots", None),
            P("wide", "shots", None),
            P("wide", "shots", None),
            P("wide", "shots", None),
            P("shots", "wide", None, None),
        ),
        check_vma=False,
    )
```

```python
import functools
import math

import jax
import jax.numpy as jnp
from jax import lax
from jax.experimental import pallas as pl
from jax.experimental.pallas import tpu as pltpu
from jax.sharding import PartitionSpec as P

REACH = 2
EDGE = 8
OUTER, INNER, CENTRE = -1.0 / 12.0, 4.0 / 3.0, -2.5
SRC, ALT = 0, 1
FIELDS = (SRC, ALT)
PARTS = 3
LEFT, RIGHT = 0, 1
MESH = pl.DeviceIdType.MESH


def second(window):
    return (
        OUTER * (window(-2) + window(2)) + INNER * (window(-1) + window(1)) + CENTRE * window(0)
    )


def window_kernel(
    devices,
    src_now_in,
    src_old_in,
    rcv_now_in,
    rcv_old_in,
    medium_in,
    wavelet_in,
    shot_in,
    traces_in,
    rec_x_in,
    lag_order_in,
    src_next,
    src_prior,
    rcv_next,
    rcv_prior,
    board,
    src_old,
    rcv_old,
    medium,
    medium_alt,
    wavelet,
    shot,
    traces,
    rec_x,
    lag_order,
    padded,
    staged,
    landed,
    waves,
    echoes,
    partial,
    partial_rcv,
    surface,
    columns,
    out_send,
    out_recv,
    halo_send,
    halo_recv,
    echo_send,
    echo_recv,
    pair_send,
    pair_recv,
    load_sems,
):
    me = lax.axis_index("wide")
    pairs = devices // 2
    pair = me // 2
    odd = lax.rem(me, 2)
    slab, cells, cells_z = rcv_old.shape
    both = 2 * slab
    steps = wavelet.shape[0]
    last = steps - 1
    rows = PARTS * both
    block = slab * rows
    inside = pl.ds(EDGE, cells)
    mine = pl.ds(odd * slab, slab)
    mine_waves = pl.ds(REACH + odd * slab, slab)
    own_echoes = pl.ds(REACH, slab)

    lags = lag_order.shape[0]
    half = (lags - 1) // 2
    far_first = sorted(range(1, devices), key=lambda distance: abs(distance - devices // 2))
    far_pairs = sorted(range(1, pairs), key=lambda distance: abs(distance - pairs // 2))

    def when_first(act):
        pl.when(odd == 0)(act)

    def when_second(act):
        pl.when(odd == 1)(act)

    loads = []
    for index, (source, target) in enumerate(
        (
            (src_now_in, waves.at[0, ALT, mine_waves, inside]),
            (src_old_in, src_old.at[mine]),
            (medium_in, medium.at[:, mine]),
            (rcv_now_in, echoes.at[0, own_echoes, inside]),
            (shot_in, shot),
            (traces_in, traces),
            (rec_x_in, rec_x),
            (rcv_old_in, rcv_old),
            (wavelet_in, wavelet),
            (lag_order_in, lag_order),
        )
    ):
        loads.append(pltpu.make_async_copy(source, target, load_sems.at[index]))
    for load in loads[:3]:
        load.start()

    barrier = pltpu.get_barrier_semaphore()

    def greet(peer):
        pl.semaphore_signal(
            barrier, inc=1, device_id={"wide": peer}, device_id_type=MESH
        )

    @when_second
    def _():
        for distance in far_first:
            greet(lax.rem(me + distance, devices))

    @when_first
    def _():
        greet(me + 1)
        pl.when(pair > 0)(lambda: greet(me - 1))

    for load in loads[3:]:
        load.start()

    zero_edge = jnp.zeros((EDGE, cells_z), jnp.float32)
    zero_plane = jnp.zeros((cells, cells_z), jnp.float32)
    zero_half = jnp.zeros((half, cells_z), jnp.float32)

    for field in FIELDS:
        for level in range(steps):
            for at in range(REACH, REACH + both):
                waves[level, field, at, 0:EDGE, :] = zero_edge
                waves[level, field, at, EDGE + cells : EDGE + cells + EDGE, :] = zero_edge
    for level in range(steps):
        for at in range(REACH, REACH + slab):
            echoes[level, at, 0:EDGE, :] = zero_edge
            echoes[level, at, EDGE + cells : EDGE + cells + EDGE, :] = zero_edge

    row_at = lax.broadcasted_iota(jnp.int32, (cells, cells_z), 0)
    lane_at = lax.broadcasted_iota(jnp.int32, (cells, cells_z), 1)

    def along_rows(plane):
        def window(shift):
            return plane(pl.ds(EDGE + shift, cells))

        return second(window)

    for load in loads[:3]:
        load.wait()
    for at in range(slab):
        def now_rows(where):
            return waves[0, ALT, REACH + odd * slab + at, where, :]

        sent_rows = (
            lambda: now_rows(inside),
            lambda: src_old[odd * slab + at],
            lambda: along_rows(now_rows),
        )
        for part, rows_of in enumerate(sent_rows):
            partial[part, at] = rows_of()
            for y in range(both):
                into = at * rows + part * both + y
                staged[SRC, pl.ds(into, pairs, stride=block), :] = partial[
                    part, at, pl.ds(y, pairs, stride=both), :
                ]
        for part in range(PARTS):
            for x in range(both):
                into = at * rows + part * both + x
                staged[ALT, pl.ds(into, pairs, stride=block), :] = medium[
                    part, odd * slab + at, pl.ds(x, pairs, stride=both), :
                ]

    pl.semaphore_wait(barrier, pairs + odd * (pair < pairs - 1).astype(jnp.int32))

    def remote(source, target, send, recv, peer):
        return pltpu.make_async_remote_copy(
            src_ref=source,
            dst_ref=target,
            send_sem=send,
            recv_sem=recv,
            device_id={"wide": peer},
            device_id_type=MESH,
        )

    def out_copy(field, to):
        return remote(
            staged.at[field, pl.ds(pl.multiple_of(to * block, 8), block)],
            landed.at[field, pl.ds(pl.multiple_of(me * block, 8), block)],
            out_send.at[field],
            out_recv.at[field],
            2 * to + 1,
        )

    def pair_copy(index):
        early = index < 3
        source = (
            waves.at[0, ALT, pl.ds(REACH, slab), inside],
            src_old.at[pl.ds(0, slab)],
            medium.at[:, pl.ds(0, slab)],
            medium_alt.at[:, pl.ds(0, slab)],
            waves.at[last - 1, :, pl.ds(REACH, slab), inside],
            waves.at[last, :, pl.ds(REACH, both), inside],
        )[index]
        peer = 2 * pair + 1 if early else 2 * pair
        return remote(source, source, pair_send.at[index], pair_recv.at[index], peer)

    def halo_copy(field, level, side):
        first = both if side == LEFT else REACH
        into = 0 if side == LEFT else REACH + both
        to = pair + 1 if side == LEFT else pair - 1
        peer = 2 * to if level == last and side == LEFT else 2 * to + 1
        return remote(
            waves.at[level, field, pl.ds(first, REACH), inside],
            waves.at[level, field, pl.ds(into, REACH), inside],
            halo_send.at[field, level, side],
            halo_recv.at[field, level, side],
            peer,
        )

    def sends_to(side):
        return pair < pairs - 1 if side == LEFT else pair > 0

    def gets_from(side):
        return pair > 0 if side == LEFT else pair < pairs - 1

    def send_halo(field, level, side):
        pl.when(sends_to(side))(lambda: halo_copy(field, level, side).start())

    def wait_sent(field, level, side):
        pl.when(sends_to(side))(lambda: halo_copy(field, level, side).wait_send())

    def wait_halo(field, level, side):
        pl.when(gets_from(side))(lambda: halo_copy(field, level, side).wait_recv())

    def echo_copy(level, side):
        first = slab if side == LEFT else REACH
        into = 0 if side == LEFT else REACH + slab
        return remote(
            echoes.at[level, pl.ds(first, REACH), inside],
            echoes.at[level, pl.ds(into, REACH), inside],
            echo_send.at[level, side],
            echo_recv.at[level, side],
            me + 1 if side == LEFT else me - 1,
        )

    def each_side(act):
        pl.when(me < devices - 1)(lambda: act(LEFT))
        pl.when(me > 0)(lambda: act(RIGHT))

    def send_echo(level):
        each_side(lambda side: echo_copy(level, side).start())

    def wait_echo(level):
        each_side(lambda side: echo_copy(level, 1 - side).wait_recv())

    loads[3].wait()
    send_echo(0)

    for field in FIELDS:
        for distance in far_pairs:
            out_copy(field, lax.rem(pair + distance, pairs)).start()

    for load in loads[4:]:
        load.wait()

    @when_first
    def _():
        for field in FIELDS:
            out_copy(field, pair).start()
        send_halo(ALT, 0, RIGHT)
        for index in range(3):
            pair_copy(index).start()

    @when_second
    def _():
        send_halo(ALT, 0, LEFT)
        own = pl.ds(pl.multiple_of(me * block, 8), block)
        for field in FIELDS:
            landed[field, own, :] = staged[
                field, pl.ds(pl.multiple_of(pair * block, 8), block), :
            ]


    for snap in range(padded.shape[0]):
        for field in range(2):
            for y in range(slab):
                padded[snap, field, y, 0:half, :] = zero_half
                padded[snap, field, y, half + cells : 2 * half + cells, :] = zero_half

    def clear_planes(first):
        for level in range(steps):
            for field in FIELDS:
                for at in range(REACH):
                    waves[level, field, first + at, inside, :] = zero_plane

    pl.when(pair == 0)(lambda: clear_planes(0))
    pl.when(pair == pairs - 1)(lambda: clear_planes(REACH + both))

    def clear_echoes(first):
        for level in range(steps):
            for at in range(REACH):
                echoes[level, first + at, inside, :] = zero_plane

    pl.when(me == 0)(lambda: clear_echoes(0))
    pl.when(me == devices - 1)(lambda: clear_echoes(REACH + slab))

    deep = lane_at == shot[2]
    columns[SRC] = ((row_at == shot[0]) & deep).astype(jnp.float32)
    columns[ALT] = ((row_at == shot[1]) & deep).astype(jnp.float32)
    x_at = lax.broadcasted_iota(jnp.int32, (cells, traces.shape[2]), 0)
    for y in range(slab):
        onehot = (x_at == rec_x[y : y + 1, :]).astype(jnp.float32)
        for step in range(steps):
            total = jnp.sum(onehot * traces[y, step : step + 1, :], axis=1, keepdims=True)
            surface[step, y] = jnp.where(lane_at == 0, total, 0.0)

    def arrived_rows(field, part, at):
        return landed[field, pl.ds(part * both + at, cells, stride=rows), :]

    def along_lanes(centre):
        def window(shift):
            if shift == 0:
                return centre
            turned = pltpu.roll(centre, (-shift) % cells_z, 1)
            kept = lane_at >= -shift if shift < 0 else lane_at < cells_z - shift
            return jnp.where(kept, turned, 0.0)

        return second(window)

    def flat(plane, older, rows_speed, lanes_speed):
        centre = plane(inside)
        return (
            2.0 * centre
            - older
            + rows_speed * along_rows(plane)
            + lanes_speed * along_lanes(centre)
        )

    def speed(field, part, at):
        if field == ALT:
            return medium_alt[part, at]
        return medium[(1, 0, 2)[part], at]

    def local(field, level, ats):
        for at in ats:
            def plane(where):
                return waves[level, field, REACH + at, where, :]

            if level > 0:
                older = waves[level - 1, field, REACH + at, inside, :]
            elif field == ALT:
                older = src_old[at]
            else:
                older = arrived_rows(SRC, 1, at)
            partial[field, at] = flat(plane, older, speed(field, 1, at), speed(field, 2, at))

    def finish(field, level, ats):
        for at in ats:
            def along_planes(shift):
                return waves[level, field, REACH + at + shift, inside, :]

            if field == SRC and level == 0:
                bend = arrived_rows(SRC, 2, at)
            else:
                bend = second(along_planes)
            hit = (pair * both + at == shot[1 if field == SRC else 0]).astype(jnp.float32)
            waves[level + 1, field, REACH + at, inside, :] = (
                partial[field, at]
                + speed(field, 0, at) * bend
                - (wavelet[level] * hit) * columns[field]
            )

    def local_both(level, ats):
        for field in FIELDS:
            local(field, level, ats)

    def local_rcv(level):
        for at in range(slab):
            def plane(where):
                return echoes[level, REACH + at, where, :]

            older = echoes[level - 1, REACH + at, inside, :] if level > 0 else rcv_old[at]
            here = odd * slab + at
            partial_rcv[at] = flat(plane, older, medium[0, here], medium[2, here])

    def finish_rcv(level):
        for at in range(slab):
            def along_planes(shift):
                return echoes[level, REACH + at + shift, inside, :]

            echoes[level + 1, REACH + at, inside, :] = (
                partial_rcv[at]
                + medium[1, odd * slab + at] * second(along_planes)
                + surface[level, at]
            )

    def keep_src(level):
        for y in range(slab):
            padded[level // 2 - 1, 0, y, half : half + cells, :] = waves[
                level, SRC, REACH + odd * slab + y, inside, :
            ]

    def keep_rcv(level):
        for y in range(slab):
            padded[level // 2 - 1, 1, y, half : half + cells, :] = echoes[
                level, REACH + y, inside, :
            ]

    def correlate(snap):
        for plane in range(lags):
            slot = lag_order[plane]
            at_src = pl.ds(2 * half - slot, cells)
            at_rcv = pl.ds(slot, cells)
            for y in range(slab):
                product = padded[snap, 0, y, at_src, :] * padded[snap, 1, y, at_rcv, :]
                board[plane, y] = product if snap == 0 else board[plane, y] + product

    everyone = range(both)
    firsts, seconds = range(slab), range(slab, both)

    def advance_rcv(level):
        wait_echo(level)
        finish_rcv(level)
        if level < last:
            send_echo(level + 1)
            local_rcv(level + 1)

    local_rcv(0)
    advance_rcv(0)

    def wait_out(field):
        arrived = landed.at[field, pl.ds(0, (devices - 1) * block)]
        pltpu.make_async_copy(arrived, arrived, out_recv.at[field]).wait()

    def begin(field):
        local(field, 0, everyone)
        finish(field, 0, everyone)
        for side in (RIGHT, LEFT):
            send_halo(field, 1, side)
        local(field, 1, everyone)

    def one_side(field, level, side):
        wait_halo(field, level, side)
        finish(field, level, firsts if side == LEFT else seconds)
        send_halo(field, level + 1, 1 - side)

    def go_on(field, level):
        for side in (LEFT, RIGHT):
            one_side(field, level, side)
        local(field, level + 1, everyone if level + 1 < last else seconds)

    @when_second
    def _():
        pair_copy(2).wait_recv()
        wait_out(SRC)
        for at in everyone:
            waves[0, SRC, REACH + at, inside, :] = arrived_rows(SRC, 0, at)
        begin(SRC)

    advance_rcv(1)

    @when_second
    def _():
        for index in range(2):
            pair_copy(index).wait_recv()
        for side in (LEFT, RIGHT):
            wait_halo(ALT, 0, side)
        wait_out(ALT)
        for at in everyone:
            for part in range(PARTS):
                medium_alt[part, at] = arrived_rows(ALT, part, at)
        begin(ALT)
        pair_copy(3).start()

    for level in range(1, last):

        @when_second
        def _():
            go_on(SRC, level)

        @when_second
        def _():
            go_on(ALT, level)
            if level + 1 == last - 1:
                pair_copy(4).start()
            if level + 1 == last:
                pair_copy(5).start()

        advance_rcv(level + 1)
    @when_first
    def _():
        for index in (3, 4):
            pair_copy(index).wait_recv()

    keep_src(2)
    keep_rcv(2)
    keep_rcv(steps)
    correlate(0)
    for at in range(slab):
        rcv_next[at] = echoes[steps, REACH + at, inside, :]
        rcv_prior[at] = echoes[last, REACH + at, inside, :]

    @when_first
    def _():
        pair_copy(5).wait_recv()
        local_both(last, firsts)

    def arrive(field):
        @when_second
        def _():
            wait_halo(field, last, RIGHT)
            finish(field, last, seconds)

        @when_first
        def _():
            wait_halo(field, last, LEFT)
            finish(field, last, firsts)

    arrive(SRC)
    keep_src(steps)
    correlate(1)
    arrive(ALT)
    for at in range(slab):
        src_next[at] = waves[steps, ALT, REACH + odd * slab + at, inside, :]
        src_prior[at] = waves[last, ALT, REACH + odd * slab + at, inside, :]

    @when_first
    def _():
        for field in FIELDS:
            sent = staged.at[field, pl.ds(0, pairs * block)]
            pltpu.make_async_copy(sent, sent, out_send.at[field]).wait()
        wait_sent(ALT, 0, RIGHT)
        for index in range(3):
            pair_copy(index).wait_send()

    @when_second
    def _():
        for field in FIELDS:
            sent = staged.at[field, pl.ds(0, (pairs - 1) * block)]
            pltpu.make_async_copy(sent, sent, out_send.at[field]).wait()
        wait_sent(ALT, 0, LEFT)
        for level in range(1, steps):
            for field in FIELDS:
                for side in (LEFT, RIGHT):
                    wait_sent(field, level, side)
        for index in range(3, 6):
            pair_copy(index).wait_send()

    for level in range(steps):
        each_side(lambda side: echo_copy(level, side).wait_send())


def deliver_kernel(*refs):
    count = (len(refs) - 1) // 2
    copies = [
        pltpu.make_async_copy(refs[i], refs[count + i], refs[-1].at[i]) for i in range(count)
    ]
    for copy in copies:
        copy.start()
    for copy in copies:
        copy.wait()


def solution(mesh):
    devices = mesh.shape["wide"]

    def on_device(
        src_now, src_old, rcv_now, rcv_old, medium, wavelet, shot, traces, rec_x, lag_order
    ):
        slab, cells, cells_z = src_now.shape
        assert rcv_now.shape == (slab, cells_z, cells) and slab >= REACH
        assert slab * devices == cells and devices % 2 == 0
        steps = wavelet.shape[0]
        lags = lag_order.shape[0]
        half = (lags - 1) // 2
        rows = 2 * PARTS * slab
        f32 = jnp.float32
        vmem = pl.BlockSpec(memory_space=pltpu.VMEM)
        hbm = pl.BlockSpec(memory_space=pltpu.HBM)
        field_shape = jax.ShapeDtypeStruct((slab, cells, cells_z), f32)
        board_shape = jax.ShapeDtypeStruct((lags, slab, cells, cells_z), f32)
        shapes = (field_shape,) * 4 + (board_shape,)
        taken = steps // 2
        turn = lambda array: jnp.swapaxes(array, -1, -2)
        like = lambda array: pltpu.VMEM(array.shape, array.dtype)
        scalars = lambda array: pltpu.SMEM(array.shape, array.dtype)
        rcv_now, rcv_old, medium, traces = map(turn, (rcv_now, rcv_old, medium, traces))
        both = 2 * slab
        field = lambda *lead: pltpu.VMEM((*lead, cells, cells_z), f32)
        wide = lambda *lead: pltpu.VMEM((*lead, cells + 2 * EDGE, cells_z), f32)
        scratch = [
            field(both),
            like(rcv_old),
            field(PARTS, both),
            field(PARTS, both),
            scalars(wavelet),
            scalars(shot),
            like(traces),
            like(rec_x),
            scalars(lag_order),
            pltpu.VMEM((taken, 2, slab, cells + 2 * half, cells_z), f32),
            pltpu.VMEM((2, devices // 2 * slab * rows, cells_z), f32),
            pltpu.VMEM((2, devices * slab * rows, cells_z), f32),
            wide(steps + 1, 2, both + 2 * REACH),
            wide(steps + 1, slab + 2 * REACH),
            field(PARTS, both),
            field(slab),
            field(steps, slab),
            field(2),
        ]
        held = sum(4 * math.prod(each.shape) for each in scratch + list(shapes))
        results = pl.pallas_call(
            functools.partial(window_kernel, devices),
            out_shape=shapes,
            in_specs=[hbm] * 10,
            out_specs=(vmem,) * 5,
            scratch_shapes=scratch
            + [pltpu.SemaphoreType.DMA((2,))] * 2
            + [pltpu.SemaphoreType.DMA((2, steps, 2))] * 2
            + [pltpu.SemaphoreType.DMA((steps, 2))] * 2
            + [pltpu.SemaphoreType.DMA((6,))] * 2
            + [pltpu.SemaphoreType.DMA((10,))],
            compiler_params=pltpu.CompilerParams(
                collective_id=0, has_side_effects=True, vmem_limit_bytes=held + (4 << 20)
            ),
            name="window",
        )(
            *(
                pltpu.with_memory_space_constraint(array, pltpu.HBM)
                for array in (
                    src_now,
                    src_old,
                    rcv_now,
                    rcv_old,
                    medium,
                    wavelet,
                    shot,
                    traces,
                    rec_x,
                    lag_order,
                )
            )
        )
        outs = pl.pallas_call(
            deliver_kernel,
            out_shape=shapes,
            in_specs=[vmem] * 5,
            out_specs=(hbm,) * 5,
            scratch_shapes=[pltpu.SemaphoreType.DMA((5,))],
            compiler_params=pltpu.CompilerParams(vmem_limit_bytes=held + (4 << 20)),
            name="deliver",
        )(*results)
        return outs[0], outs[1], turn(outs[2]), turn(outs[3]), turn(outs[4])

    return jax.shard_map(
        on_device,
        mesh=mesh,
        in_specs=(
            P("wide", "shots", None),
            P("wide", "shots", None),
            P("wide", "shots", None),
            P("wide", "shots", None),
            P(None, "wide", None, None),
            P(),
            P("shots"),
            P("wide", "shots", None),
            P("wide", "shots"),
            P(),
        ),
        out_specs=(
            P("wide", "shots", None),
            P("wide", "shots", None),
            P("wide", "shots", None),
            P("wide", "shots", None),
            P("shots", "wide", None, None),
        ),
        check_vma=False,
    )
```

```python
import functools
import math

import jax
import jax.numpy as jnp
from jax import lax
from jax.experimental import pallas as pl
from jax.experimental.pallas import tpu as pltpu
from jax.sharding import PartitionSpec as P

REACH = 2
EDGE = 8
OUTER, INNER, CENTRE = -1.0 / 12.0, 4.0 / 3.0, -2.5
SRC, ALT = 0, 1
FIELDS = (SRC, ALT)
PARTS = 3
LEFT, RIGHT = 0, 1
MESH = pl.DeviceIdType.MESH


def second(window):
    return (
        OUTER * (window(-2) + window(2)) + INNER * (window(-1) + window(1)) + CENTRE * window(0)
    )


def window_kernel(
    devices,
    src_now_in,
    src_old_in,
    rcv_now_in,
    rcv_old_in,
    medium_in,
    wavelet_in,
    shot_in,
    traces_in,
    rec_x_in,
    lag_order_in,
    src_next,
    src_prior,
    rcv_next,
    rcv_prior,
    board,
    src_old,
    rcv_old,
    medium,
    medium_alt,
    wavelet,
    shot,
    traces,
    rec_x,
    lag_order,
    padded,
    staged,
    landed,
    waves,
    echoes,
    partial,
    partial_rcv,
    surface,
    columns,
    out_send,
    out_recv,
    halo_send,
    halo_recv,
    echo_send,
    echo_recv,
    pair_send,
    pair_recv,
    load_sems,
):
    me = lax.axis_index("wide")
    pairs = devices // 2
    pair = me // 2
    odd = lax.rem(me, 2)
    slab, cells, cells_z = rcv_old.shape
    both = 2 * slab
    steps = wavelet.shape[0]
    last = steps - 1
    rows = PARTS * both
    block = slab * rows
    inside = pl.ds(EDGE, cells)
    mine = pl.ds(odd * slab, slab)
    mine_waves = pl.ds(REACH + odd * slab, slab)
    own_echoes = pl.ds(REACH, slab)

    lags = lag_order.shape[0]
    half = (lags - 1) // 2
    far_first = sorted(range(1, devices), key=lambda distance: abs(distance - devices // 2))
    far_pairs = sorted(range(1, pairs), key=lambda distance: abs(distance - pairs // 2))

    def when_first(act):
        pl.when(odd == 0)(act)

    def when_second(act):
        pl.when(odd == 1)(act)

    loads = []
    for index, (source, target) in enumerate(
        (
            (src_now_in, waves.at[0, ALT, mine_waves, inside]),
            (src_old_in, src_old.at[mine]),
            (medium_in, medium.at[:, mine]),
            (rcv_now_in, echoes.at[0, own_echoes, inside]),
            (shot_in, shot),
            (traces_in, traces),
            (rec_x_in, rec_x),
            (rcv_old_in, rcv_old),
            (wavelet_in, wavelet),
            (lag_order_in, lag_order),
        )
    ):
        loads.append(pltpu.make_async_copy(source, target, load_sems.at[index]))
    for load in loads[:3]:
        load.start()

    barrier = pltpu.get_barrier_semaphore()

    def greet(peer):
        pl.semaphore_signal(
            barrier, inc=1, device_id={"wide": peer}, device_id_type=MESH
        )

    @when_second
    def _():
        for distance in far_first:
            greet(lax.rem(me + distance, devices))

    @when_first
    def _():
        greet(me + 1)
        pl.when(pair > 0)(lambda: greet(me - 1))

    for load in loads[3:]:
        load.start()

    zero_edge = jnp.zeros((EDGE, cells_z), jnp.float32)
    zero_plane = jnp.zeros((cells, cells_z), jnp.float32)
    zero_half = jnp.zeros((half, cells_z), jnp.float32)

    for field in FIELDS:
        for level in range(steps):
            for at in range(REACH, REACH + both):
                waves[level, field, at, 0:EDGE, :] = zero_edge
                waves[level, field, at, EDGE + cells : EDGE + cells + EDGE, :] = zero_edge
    for level in range(steps):
        for at in range(REACH, REACH + slab):
            echoes[level, at, 0:EDGE, :] = zero_edge
            echoes[level, at, EDGE + cells : EDGE + cells + EDGE, :] = zero_edge

    row_at = lax.broadcasted_iota(jnp.int32, (cells, cells_z), 0)
    lane_at = lax.broadcasted_iota(jnp.int32, (cells, cells_z), 1)

    def along_rows(plane):
        def window(shift):
            return plane(pl.ds(EDGE + shift, cells))

        return second(window)

    for load in loads[:2]:
        load.wait()
    for at in range(slab):
        def now_rows(where):
            return waves[0, ALT, REACH + odd * slab + at, where, :]

        sent_rows = (
            lambda: now_rows(inside),
            lambda: src_old[odd * slab + at],
            lambda: along_rows(now_rows),
        )
        for part, rows_of in enumerate(sent_rows):
            partial[part, at] = rows_of()
            for y in range(both):
                into = at * rows + part * both + y
                staged[SRC, pl.ds(into, pairs, stride=block), :] = partial[
                    part, at, pl.ds(y, pairs, stride=both), :
                ]

    pl.semaphore_wait(barrier, pairs + odd * (pair < pairs - 1).astype(jnp.int32))

    def remote(source, target, send, recv, peer):
        return pltpu.make_async_remote_copy(
            src_ref=source,
            dst_ref=target,
            send_sem=send,
            recv_sem=recv,
            device_id={"wide": peer},
            device_id_type=MESH,
        )

    def out_copy(field, to):
        return remote(
            staged.at[field, pl.ds(pl.multiple_of(to * block, 8), block)],
            landed.at[field, pl.ds(pl.multiple_of(me * block, 8), block)],
            out_send.at[field],
            out_recv.at[field],
            2 * to + 1,
        )

    def pair_copy(index):
        early = index < 3
        source = (
            waves.at[0, ALT, pl.ds(REACH, slab), inside],
            src_old.at[pl.ds(0, slab)],
            medium.at[:, pl.ds(0, slab)],
            medium_alt.at[:, pl.ds(0, slab)],
            waves.at[last - 1, :, pl.ds(REACH, slab), inside],
            waves.at[last, :, pl.ds(REACH, both), inside],
        )[index]
        peer = 2 * pair + 1 if early else 2 * pair
        return remote(source, source, pair_send.at[index], pair_recv.at[index], peer)

    def halo_copy(field, level, side):
        first = both if side == LEFT else REACH
        into = 0 if side == LEFT else REACH + both
        to = pair + 1 if side == LEFT else pair - 1
        peer = 2 * to if level == last and side == LEFT else 2 * to + 1
        return remote(
            waves.at[level, field, pl.ds(first, REACH), inside],
            waves.at[level, field, pl.ds(into, REACH), inside],
            halo_send.at[field, level, side],
            halo_recv.at[field, level, side],
            peer,
        )

    def sends_to(side):
        return pair < pairs - 1 if side == LEFT else pair > 0

    def gets_from(side):
        return pair > 0 if side == LEFT else pair < pairs - 1

    def send_halo(field, level, side):
        pl.when(sends_to(side))(lambda: halo_copy(field, level, side).start())

    def wait_sent(field, level, side):
        pl.when(sends_to(side))(lambda: halo_copy(field, level, side).wait_send())

    def wait_halo(field, level, side):
        pl.when(gets_from(side))(lambda: halo_copy(field, level, side).wait_recv())

    def echo_copy(level, side):
        first = slab if side == LEFT else REACH
        into = 0 if side == LEFT else REACH + slab
        return remote(
            echoes.at[level, pl.ds(first, REACH), inside],
            echoes.at[level, pl.ds(into, REACH), inside],
            echo_send.at[level, side],
            echo_recv.at[level, side],
            me + 1 if side == LEFT else me - 1,
        )

    def each_side(act):
        pl.when(me < devices - 1)(lambda: act(LEFT))
        pl.when(me > 0)(lambda: act(RIGHT))

    def send_echo(level):
        each_side(lambda side: echo_copy(level, side).start())

    def wait_echo(level):
        each_side(lambda side: echo_copy(level, 1 - side).wait_recv())

    loads[3].wait()
    send_echo(0)

    def send_out(field):
        for distance in far_pairs[::-1]:
            out_copy(field, lax.rem(pair + distance, pairs)).start()

    send_out(SRC)
    loads[2].wait()
    for at in range(slab):
        for part in range(PARTS):
            for x in range(both):
                into = at * rows + part * both + x
                staged[ALT, pl.ds(into, pairs, stride=block), :] = medium[
                    part, odd * slab + at, pl.ds(x, pairs, stride=both), :
                ]
    send_out(ALT)

    for load in loads[4:]:
        load.wait()

    @when_first
    def _():
        for field in FIELDS:
            out_copy(field, pair).start()
        send_halo(ALT, 0, RIGHT)
        for index in range(3):
            pair_copy(index).start()

    @when_second
    def _():
        send_halo(ALT, 0, LEFT)
        own = pl.ds(pl.multiple_of(me * block, 8), block)
        for field in FIELDS:
            landed[field, own, :] = staged[
                field, pl.ds(pl.multiple_of(pair * block, 8), block), :
            ]


    for snap in range(padded.shape[0]):
        for field in range(2):
            for y in range(slab):
                padded[snap, field, y, 0:half, :] = zero_half
                padded[snap, field, y, half + cells : 2 * half + cells, :] = zero_half

    def clear_planes(first):
        for level in range(steps):
            for field in FIELDS:
                for at in range(REACH):
                    waves[level, field, first + at, inside, :] = zero_plane

    pl.when(pair == 0)(lambda: clear_planes(0))
    pl.when(pair == pairs - 1)(lambda: clear_planes(REACH + both))

    def clear_echoes(first):
        for level in range(steps):
            for at in range(REACH):
                echoes[level, first + at, inside, :] = zero_plane

    pl.when(me == 0)(lambda: clear_echoes(0))
    pl.when(me == devices - 1)(lambda: clear_echoes(REACH + slab))

    deep = lane_at == shot[2]
    columns[SRC] = ((row_at == shot[0]) & deep).astype(jnp.float32)
    columns[ALT] = ((row_at == shot[1]) & deep).astype(jnp.float32)
    x_at = lax.broadcasted_iota(jnp.int32, (cells, traces.shape[2]), 0)
    for y in range(slab):
        onehot = (x_at == rec_x[y : y + 1, :]).astype(jnp.float32)
        for step in range(steps):
            total = jnp.sum(onehot * traces[y, step : step + 1, :], axis=1, keepdims=True)
            surface[step, y] = jnp.where(lane_at == 0, total, 0.0)

    def arrived_rows(field, part, at):
        return landed[field, pl.ds(part * both + at, cells, stride=rows), :]

    def along_lanes(centre):
        def window(shift):
            if shift == 0:
                return centre
            turned = pltpu.roll(centre, (-shift) % cells_z, 1)
            kept = lane_at >= -shift if shift < 0 else lane_at < cells_z - shift
            return jnp.where(kept, turned, 0.0)

        return second(window)

    def flat(plane, older, rows_speed, lanes_speed):
        centre = plane(inside)
        return (
            2.0 * centre
            - older
            + rows_speed * along_rows(plane)
            + lanes_speed * along_lanes(centre)
        )

    def speed(field, part, at):
        if field == ALT:
            return medium_alt[part, at]
        return medium[(1, 0, 2)[part], at]

    def local(field, level, ats):
        for at in ats:
            def plane(where):
                return waves[level, field, REACH + at, where, :]

            if level > 0:
                older = waves[level - 1, field, REACH + at, inside, :]
            elif field == ALT:
                older = src_old[at]
            else:
                older = arrived_rows(SRC, 1, at)
            partial[field, at] = flat(plane, older, speed(field, 1, at), speed(field, 2, at))

    def finish(field, level, ats):
        for at in ats:
            def along_planes(shift):
                return waves[level, field, REACH + at + shift, inside, :]

            if field == SRC and level == 0:
                bend = arrived_rows(SRC, 2, at)
            else:
                bend = second(along_planes)
            hit = (pair * both + at == shot[1 if field == SRC else 0]).astype(jnp.float32)
            waves[level + 1, field, REACH + at, inside, :] = (
                partial[field, at]
                + speed(field, 0, at) * bend
                - (wavelet[level] * hit) * columns[field]
            )

    def local_both(level, ats):
        for field in FIELDS:
            local(field, level, ats)

    def local_rcv(level):
        for at in range(slab):
            def plane(where):
                return echoes[level, REACH + at, where, :]

            older = echoes[level - 1, REACH + at, inside, :] if level > 0 else rcv_old[at]
            here = odd * slab + at
            partial_rcv[at] = flat(plane, older, medium[0, here], medium[2, here])

    def finish_rcv(level):
        for at in range(slab):
            def along_planes(shift):
                return echoes[level, REACH + at + shift, inside, :]

            echoes[level + 1, REACH + at, inside, :] = (
                partial_rcv[at]
                + medium[1, odd * slab + at] * second(along_planes)
                + surface[level, at]
            )

    def keep_src(level):
        for y in range(slab):
            padded[level // 2 - 1, 0, y, half : half + cells, :] = waves[
                level, SRC, REACH + odd * slab + y, inside, :
            ]

    def keep_rcv(level):
        for y in range(slab):
            padded[level // 2 - 1, 1, y, half : half + cells, :] = echoes[
                level, REACH + y, inside, :
            ]

    def correlate(snap):
        for plane in range(lags):
            slot = lag_order[plane]
            at_src = pl.ds(2 * half - slot, cells)
            at_rcv = pl.ds(slot, cells)
            for y in range(slab):
                product = padded[snap, 0, y, at_src, :] * padded[snap, 1, y, at_rcv, :]
                board[plane, y] = product if snap == 0 else board[plane, y] + product

    everyone = range(both)
    firsts, seconds = range(slab), range(slab, both)

    def advance_rcv(level):
        wait_echo(level)
        finish_rcv(level)
        if level < last:
            send_echo(level + 1)
            local_rcv(level + 1)

    local_rcv(0)
    advance_rcv(0)

    def wait_out(field):
        arrived = landed.at[field, pl.ds(0, (devices - 1) * block)]
        pltpu.make_async_copy(arrived, arrived, out_recv.at[field]).wait()

    def begin(field):
        for side, ats in ((RIGHT, firsts), (LEFT, seconds)):
            local(field, 0, ats)
            finish(field, 0, ats)
            send_halo(field, 1, side)
        local(field, 1, everyone)

    def one_side(field, level, side):
        wait_halo(field, level, side)
        finish(field, level, firsts if side == LEFT else seconds)
        send_halo(field, level + 1, 1 - side)

    def go_on(field, level):
        for side in (LEFT, RIGHT):
            one_side(field, level, side)
        local(field, level + 1, everyone if level + 1 < last else seconds)

    @when_second
    def _():
        pair_copy(2).wait_recv()
        wait_out(SRC)
        for at in everyone:
            waves[0, SRC, REACH + at, inside, :] = arrived_rows(SRC, 0, at)
        begin(SRC)

    advance_rcv(1)

    @when_second
    def _():
        for index in range(2):
            pair_copy(index).wait_recv()
        for side in (LEFT, RIGHT):
            wait_halo(ALT, 0, side)
        wait_out(ALT)
        for at in everyone:
            for part in range(PARTS):
                medium_alt[part, at] = arrived_rows(ALT, part, at)
        begin(ALT)
        pair_copy(3).start()

    for level in range(1, last):

        @when_second
        def _():
            go_on(SRC, level)

        @when_second
        def _():
            go_on(ALT, level)
            if level + 1 == last - 1:
                pair_copy(4).start()
            if level + 1 == last:
                pair_copy(5).start()
            for side in (LEFT, RIGHT):
                wait_sent(ALT, level + 1, side)

        advance_rcv(level + 1)
    @when_first
    def _():
        for index in (3, 4):
            pair_copy(index).wait_recv()

    keep_src(2)
    keep_rcv(2)
    keep_rcv(steps)
    correlate(0)
    for at in range(slab):
        rcv_next[at] = echoes[steps, REACH + at, inside, :]
        rcv_prior[at] = echoes[last, REACH + at, inside, :]

    @when_first
    def _():
        pair_copy(5).wait_recv()
        local_both(last, firsts)

    def arrive(field):
        @when_second
        def _():
            wait_halo(field, last, RIGHT)
            finish(field, last, seconds)

        @when_first
        def _():
            wait_halo(field, last, LEFT)
            finish(field, last, firsts)

    arrive(SRC)
    keep_src(steps)
    correlate(1)
    arrive(ALT)
    for at in range(slab):
        src_next[at] = waves[steps, ALT, REACH + odd * slab + at, inside, :]
        src_prior[at] = waves[last, ALT, REACH + odd * slab + at, inside, :]

    @when_first
    def _():
        for field in FIELDS:
            sent = staged.at[field, pl.ds(0, pairs * block)]
            pltpu.make_async_copy(sent, sent, out_send.at[field]).wait()
        wait_sent(ALT, 0, RIGHT)
        for index in range(3):
            pair_copy(index).wait_send()

    @when_second
    def _():
        for field in FIELDS:
            sent = staged.at[field, pl.ds(0, (pairs - 1) * block)]
            pltpu.make_async_copy(sent, sent, out_send.at[field]).wait()
        wait_sent(ALT, 0, LEFT)
        for side in (LEFT, RIGHT):
            wait_sent(ALT, 1, side)
            for level in range(1, steps):
                wait_sent(SRC, level, side)
        for index in range(3, 6):
            pair_copy(index).wait_send()

    for level in range(steps):
        each_side(lambda side: echo_copy(level, side).wait_send())


def deliver_kernel(*refs):
    count = (len(refs) - 1) // 2
    copies = [
        pltpu.make_async_copy(refs[i], refs[count + i], refs[-1].at[i]) for i in range(count)
    ]
    for copy in copies:
        copy.start()
    for copy in copies:
        copy.wait()


def solution(mesh):
    devices = mesh.shape["wide"]

    def on_device(
        src_now, src_old, rcv_now, rcv_old, medium, wavelet, shot, traces, rec_x, lag_order
    ):
        slab, cells, cells_z = src_now.shape
        assert rcv_now.shape == (slab, cells_z, cells) and slab >= REACH
        assert slab * devices == cells and devices % 2 == 0
        steps = wavelet.shape[0]
        lags = lag_order.shape[0]
        half = (lags - 1) // 2
        rows = 2 * PARTS * slab
        f32 = jnp.float32
        vmem = pl.BlockSpec(memory_space=pltpu.VMEM)
        hbm = pl.BlockSpec(memory_space=pltpu.HBM)
        field_shape = jax.ShapeDtypeStruct((slab, cells, cells_z), f32)
        board_shape = jax.ShapeDtypeStruct((lags, slab, cells, cells_z), f32)
        shapes = (field_shape,) * 4 + (board_shape,)
        taken = steps // 2
        turn = lambda array: jnp.swapaxes(array, -1, -2)
        like = lambda array: pltpu.VMEM(array.shape, array.dtype)
        scalars = lambda array: pltpu.SMEM(array.shape, array.dtype)
        rcv_now, rcv_old, medium, traces = map(turn, (rcv_now, rcv_old, medium, traces))
        both = 2 * slab
        field = lambda *lead: pltpu.VMEM((*lead, cells, cells_z), f32)
        wide = lambda *lead: pltpu.VMEM((*lead, cells + 2 * EDGE, cells_z), f32)
        scratch = [
            field(both),
            like(rcv_old),
            field(PARTS, both),
            field(PARTS, both),
            scalars(wavelet),
            scalars(shot),
            like(traces),
            like(rec_x),
            scalars(lag_order),
            pltpu.VMEM((taken, 2, slab, cells + 2 * half, cells_z), f32),
            pltpu.VMEM((2, devices // 2 * slab * rows, cells_z), f32),
            pltpu.VMEM((2, devices * slab * rows, cells_z), f32),
            wide(steps + 1, 2, both + 2 * REACH),
            wide(steps + 1, slab + 2 * REACH),
            field(PARTS, both),
            field(slab),
            field(steps, slab),
            field(2),
        ]
        held = sum(4 * math.prod(each.shape) for each in scratch + list(shapes))
        results = pl.pallas_call(
            functools.partial(window_kernel, devices),
            out_shape=shapes,
            in_specs=[hbm] * 10,
            out_specs=(vmem,) * 5,
            scratch_shapes=scratch
            + [pltpu.SemaphoreType.DMA((2,))] * 2
            + [pltpu.SemaphoreType.DMA((2, steps, 2))] * 2
            + [pltpu.SemaphoreType.DMA((steps, 2))] * 2
            + [pltpu.SemaphoreType.DMA((6,))] * 2
            + [pltpu.SemaphoreType.DMA((10,))],
            compiler_params=pltpu.CompilerParams(
                collective_id=0, has_side_effects=True, vmem_limit_bytes=held + (4 << 20)
            ),
            name="window",
        )(
            *(
                pltpu.with_memory_space_constraint(array, pltpu.HBM)
                for array in (
                    src_now,
                    src_old,
                    rcv_now,
                    rcv_old,
                    medium,
                    wavelet,
                    shot,
                    traces,
                    rec_x,
                    lag_order,
                )
            )
        )
        outs = pl.pallas_call(
            deliver_kernel,
            out_shape=shapes,
            in_specs=[vmem] * 5,
            out_specs=(hbm,) * 5,
            scratch_shapes=[pltpu.SemaphoreType.DMA((5,))],
            compiler_params=pltpu.CompilerParams(vmem_limit_bytes=held + (4 << 20)),
            name="deliver",
        )(*results)
        return outs[0], outs[1], turn(outs[2]), turn(outs[3]), turn(outs[4])

    return jax.shard_map(
        on_device,
        mesh=mesh,
        in_specs=(
            P("wide", "shots", None),
            P("wide", "shots", None),
            P("wide", "shots", None),
            P("wide", "shots", None),
            P(None, "wide", None, None),
            P(),
            P("shots"),
            P("wide", "shots", None),
            P("wide", "shots"),
            P(),
        ),
        out_specs=(
            P("wide", "shots", None),
            P("wide", "shots", None),
            P("wide", "shots", None),
            P("wide", "shots", None),
            P("shots", "wide", None, None),
        ),
        check_vma=False,
    )
```

```python
import functools
import math

import jax
import jax.numpy as jnp
from jax import lax
from jax.experimental import pallas as pl
from jax.experimental.pallas import tpu as pltpu
from jax.sharding import PartitionSpec as P

REACH = 2
EDGE = 8
OUTER, INNER, CENTRE = -1.0 / 12.0, 4.0 / 3.0, -2.5
SRC, ALT = 0, 1
FIELDS = (SRC, ALT)
PARTS = 3
LEFT, RIGHT = 0, 1
MESH = pl.DeviceIdType.MESH


def second(window):
    return (
        OUTER * (window(-2) + window(2)) + INNER * (window(-1) + window(1)) + CENTRE * window(0)
    )


def window_kernel(
    devices,
    src_now_in,
    src_old_in,
    rcv_now_in,
    rcv_old_in,
    medium_in,
    wavelet_in,
    shot_in,
    traces_in,
    rec_x_in,
    lag_order_in,
    src_next,
    src_prior,
    rcv_next,
    rcv_prior,
    board,
    src_old,
    rcv_old,
    medium,
    medium_alt,
    wavelet,
    shot,
    traces,
    rec_x,
    lag_order,
    padded,
    staged,
    landed,
    waves,
    echoes,
    partial,
    partial_rcv,
    surface,
    columns,
    out_send,
    out_recv,
    halo_send,
    halo_recv,
    echo_send,
    echo_recv,
    pair_send,
    pair_recv,
    load_sems,
):
    me = lax.axis_index("wide")
    pairs = devices // 2
    pair = me // 2
    odd = lax.rem(me, 2)
    slab, cells, cells_z = rcv_old.shape
    both = 2 * slab
    steps = wavelet.shape[0]
    last = steps - 1
    rows = PARTS * both
    block = slab * rows
    inside = pl.ds(EDGE, cells)
    mine = pl.ds(odd * slab, slab)
    mine_waves = pl.ds(REACH + odd * slab, slab)
    own_echoes = pl.ds(REACH, slab)

    lags = lag_order.shape[0]
    half = (lags - 1) // 2
    far_first = sorted(range(1, devices), key=lambda distance: abs(distance - devices // 2))
    far_pairs = sorted(range(1, pairs), key=lambda distance: abs(distance - pairs // 2))

    def when_first(act):
        pl.when(odd == 0)(act)

    def when_second(act):
        pl.when(odd == 1)(act)

    loads = []
    for index, (source, target) in enumerate(
        (
            (src_now_in, waves.at[0, ALT, mine_waves, inside]),
            (src_old_in, src_old.at[mine]),
            (medium_in, medium.at[:, mine]),
            (rcv_now_in, echoes.at[0, own_echoes, inside]),
            (shot_in, shot),
            (traces_in, traces),
            (rec_x_in, rec_x),
            (rcv_old_in, rcv_old),
            (wavelet_in, wavelet),
            (lag_order_in, lag_order),
        )
    ):
        loads.append(pltpu.make_async_copy(source, target, load_sems.at[index]))
    for load in loads[:3]:
        load.start()

    barrier = pltpu.get_barrier_semaphore()

    def greet(peer):
        pl.semaphore_signal(
            barrier, inc=1, device_id={"wide": peer}, device_id_type=MESH
        )

    @when_second
    def _():
        for distance in far_first:
            greet(lax.rem(me + distance, devices))

    @when_first
    def _():
        greet(me + 1)
        pl.when(pair > 0)(lambda: greet(me - 1))

    for load in loads[3:]:
        load.start()

    zero_edge = jnp.zeros((EDGE, cells_z), jnp.float32)
    zero_plane = jnp.zeros((cells, cells_z), jnp.float32)
    zero_half = jnp.zeros((half, cells_z), jnp.float32)

    for at in range(REACH, REACH + both):
        waves[0, ALT, at, 0:EDGE, :] = zero_edge
        waves[0, ALT, at, EDGE + cells : EDGE + cells + EDGE, :] = zero_edge

    row_at = lax.broadcasted_iota(jnp.int32, (cells, cells_z), 0)
    lane_at = lax.broadcasted_iota(jnp.int32, (cells, cells_z), 1)

    def along_rows(plane):
        def window(shift):
            return plane(pl.ds(EDGE + shift, cells))

        return second(window)

    for load in loads[:2]:
        load.wait()
    for at in range(slab):
        def now_rows(where):
            return waves[0, ALT, REACH + odd * slab + at, where, :]

        sent_rows = (
            lambda: now_rows(inside),
            lambda: src_old[odd * slab + at],
            lambda: along_rows(now_rows),
        )
        for part, rows_of in enumerate(sent_rows):
            partial[part, at] = rows_of()
            for y in range(both):
                into = at * rows + part * both + y
                staged[SRC, pl.ds(into, pairs, stride=block), :] = partial[
                    part, at, pl.ds(y, pairs, stride=both), :
                ]

    pl.semaphore_wait(barrier, pairs + odd * (pair < pairs - 1).astype(jnp.int32))

    def remote(source, target, send, recv, peer):
        return pltpu.make_async_remote_copy(
            src_ref=source,
            dst_ref=target,
            send_sem=send,
            recv_sem=recv,
            device_id={"wide": peer},
            device_id_type=MESH,
        )

    def out_copy(field, to):
        return remote(
            staged.at[field, pl.ds(pl.multiple_of(to * block, 8), block)],
            landed.at[field, pl.ds(pl.multiple_of(me * block, 8), block)],
            out_send.at[field],
            out_recv.at[field],
            2 * to + 1,
        )

    def pair_copy(index):
        early = index < 3
        source = (
            waves.at[0, ALT, pl.ds(REACH, slab), inside],
            src_old.at[pl.ds(0, slab)],
            medium.at[:, pl.ds(0, slab)],
            medium_alt.at[:, pl.ds(0, slab)],
            waves.at[last - 1, :, pl.ds(REACH, slab), inside],
            waves.at[last, :, pl.ds(REACH, both), inside],
        )[index]
        peer = 2 * pair + 1 if early else 2 * pair
        return remote(source, source, pair_send.at[index], pair_recv.at[index], peer)

    def halo_copy(field, level, side):
        first = both if side == LEFT else REACH
        into = 0 if side == LEFT else REACH + both
        to = pair + 1 if side == LEFT else pair - 1
        peer = 2 * to if level == last and side == LEFT else 2 * to + 1
        return remote(
            waves.at[level, field, pl.ds(first, REACH), inside],
            waves.at[level, field, pl.ds(into, REACH), inside],
            halo_send.at[field, level, side],
            halo_recv.at[field, level, side],
            peer,
        )

    def sends_to(side):
        return pair < pairs - 1 if side == LEFT else pair > 0

    def gets_from(side):
        return pair > 0 if side == LEFT else pair < pairs - 1

    def send_halo(field, level, side):
        pl.when(sends_to(side))(lambda: halo_copy(field, level, side).start())

    def wait_sent(field, level, side):
        pl.when(sends_to(side))(lambda: halo_copy(field, level, side).wait_send())

    def wait_halo(field, level, side):
        pl.when(gets_from(side))(lambda: halo_copy(field, level, side).wait_recv())

    def echo_copy(level, side):
        first = slab if side == LEFT else REACH
        into = 0 if side == LEFT else REACH + slab
        return remote(
            echoes.at[level, pl.ds(first, REACH), inside],
            echoes.at[level, pl.ds(into, REACH), inside],
            echo_send.at[level, side],
            echo_recv.at[level, side],
            me + 1 if side == LEFT else me - 1,
        )

    def each_side(act):
        pl.when(me < devices - 1)(lambda: act(LEFT))
        pl.when(me > 0)(lambda: act(RIGHT))

    def send_echo(level):
        each_side(lambda side: echo_copy(level, side).start())

    def wait_echo(level):
        each_side(lambda side: echo_copy(level, 1 - side).wait_recv())

    loads[3].wait()
    send_echo(0)

    def send_out(field):
        for distance in far_pairs[::-1]:
            out_copy(field, lax.rem(pair + distance, pairs)).start()

    send_out(SRC)
    loads[2].wait()
    for at in range(slab):
        for part in range(PARTS):
            for x in range(both):
                into = at * rows + part * both + x
                staged[ALT, pl.ds(into, pairs, stride=block), :] = medium[
                    part, odd * slab + at, pl.ds(x, pairs, stride=both), :
                ]
    send_out(ALT)

    for field in FIELDS:
        for level in range(steps):
            for at in range(REACH, REACH + both):
                waves[level, field, at, 0:EDGE, :] = zero_edge
                waves[level, field, at, EDGE + cells : EDGE + cells + EDGE, :] = zero_edge
    for level in range(steps):
        for at in range(REACH, REACH + slab):
            echoes[level, at, 0:EDGE, :] = zero_edge
            echoes[level, at, EDGE + cells : EDGE + cells + EDGE, :] = zero_edge

    for load in loads[4:]:
        load.wait()

    @when_first
    def _():
        for field in FIELDS:
            out_copy(field, pair).start()
        send_halo(ALT, 0, RIGHT)
        for index in range(3):
            pair_copy(index).start()

    @when_second
    def _():
        send_halo(ALT, 0, LEFT)
        own = pl.ds(pl.multiple_of(me * block, 8), block)
        for field in FIELDS:
            landed[field, own, :] = staged[
                field, pl.ds(pl.multiple_of(pair * block, 8), block), :
            ]


    for snap in range(padded.shape[0]):
        for field in range(2):
            for y in range(slab):
                padded[snap, field, y, 0:half, :] = zero_half
                padded[snap, field, y, half + cells : 2 * half + cells, :] = zero_half

    def clear_planes(first):
        for level in range(steps):
            for field in FIELDS:
                for at in range(REACH):
                    waves[level, field, first + at, inside, :] = zero_plane

    pl.when(pair == 0)(lambda: clear_planes(0))
    pl.when(pair == pairs - 1)(lambda: clear_planes(REACH + both))

    def clear_echoes(first):
        for level in range(steps):
            for at in range(REACH):
                echoes[level, first + at, inside, :] = zero_plane

    pl.when(me == 0)(lambda: clear_echoes(0))
    pl.when(me == devices - 1)(lambda: clear_echoes(REACH + slab))

    deep = lane_at == shot[2]
    columns[SRC] = ((row_at == shot[0]) & deep).astype(jnp.float32)
    columns[ALT] = ((row_at == shot[1]) & deep).astype(jnp.float32)
    x_at = lax.broadcasted_iota(jnp.int32, (cells, traces.shape[2]), 0)
    for y in range(slab):
        onehot = (x_at == rec_x[y : y + 1, :]).astype(jnp.float32)
        for step in range(steps):
            total = jnp.sum(onehot * traces[y, step : step + 1, :], axis=1, keepdims=True)
            surface[step, y] = jnp.where(lane_at == 0, total, 0.0)

    def arrived_rows(field, part, at):
        return landed[field, pl.ds(part * both + at, cells, stride=rows), :]

    def along_lanes(centre):
        def window(shift):
            if shift == 0:
                return centre
            turned = pltpu.roll(centre, (-shift) % cells_z, 1)
            kept = lane_at >= -shift if shift < 0 else lane_at < cells_z - shift
            return jnp.where(kept, turned, 0.0)

        return second(window)

    def flat(plane, older, rows_speed, lanes_speed):
        centre = plane(inside)
        return (
            2.0 * centre
            - older
            + rows_speed * along_rows(plane)
            + lanes_speed * along_lanes(centre)
        )

    def speed(field, part, at):
        if field == ALT:
            return medium_alt[part, at]
        return medium[(1, 0, 2)[part], at]

    def local(field, level, ats):
        for at in ats:
            def plane(where):
                return waves[level, field, REACH + at, where, :]

            if level > 0:
                older = waves[level - 1, field, REACH + at, inside, :]
            elif field == ALT:
                older = src_old[at]
            else:
                older = arrived_rows(SRC, 1, at)
            partial[field, at] = flat(plane, older, speed(field, 1, at), speed(field, 2, at))

    def finish(field, level, ats):
        for at in ats:
            def along_planes(shift):
                return waves[level, field, REACH + at + shift, inside, :]

            if field == SRC and level == 0:
                bend = arrived_rows(SRC, 2, at)
            else:
                bend = second(along_planes)
            hit = (pair * both + at == shot[1 if field == SRC else 0]).astype(jnp.float32)
            waves[level + 1, field, REACH + at, inside, :] = (
                partial[field, at]
                + speed(field, 0, at) * bend
                - (wavelet[level] * hit) * columns[field]
            )

    def local_both(level, ats):
        for field in FIELDS:
            local(field, level, ats)

    def local_rcv(level):
        for at in range(slab):
            def plane(where):
                return echoes[level, REACH + at, where, :]

            older = echoes[level - 1, REACH + at, inside, :] if level > 0 else rcv_old[at]
            here = odd * slab + at
            partial_rcv[at] = flat(plane, older, medium[0, here], medium[2, here])

    def finish_rcv(level):
        for at in range(slab):
            def along_planes(shift):
                return echoes[level, REACH + at + shift, inside, :]

            echoes[level + 1, REACH + at, inside, :] = (
                partial_rcv[at]
                + medium[1, odd * slab + at] * second(along_planes)
                + surface[level, at]
            )

    def keep_src(level):
        for y in range(slab):
            padded[level // 2 - 1, 0, y, half : half + cells, :] = waves[
                level, SRC, REACH + odd * slab + y, inside, :
            ]

    def keep_rcv(level):
        for y in range(slab):
            padded[level // 2 - 1, 1, y, half : half + cells, :] = echoes[
                level, REACH + y, inside, :
            ]

    def correlate(snap):
        for plane in range(lags):
            slot = lag_order[plane]
            at_src = pl.ds(2 * half - slot, cells)
            at_rcv = pl.ds(slot, cells)
            for y in range(slab):
                product = padded[snap, 0, y, at_src, :] * padded[snap, 1, y, at_rcv, :]
                board[plane, y] = product if snap == 0 else board[plane, y] + product

    everyone = range(both)
    firsts, seconds = range(slab), range(slab, both)

    def advance_rcv(level):
        wait_echo(level)
        finish_rcv(level)
        if level < last:
            send_echo(level + 1)
            local_rcv(level + 1)

    local_rcv(0)
    advance_rcv(0)

    def wait_out(field):
        arrived = landed.at[field, pl.ds(0, (devices - 1) * block)]
        pltpu.make_async_copy(arrived, arrived, out_recv.at[field]).wait()

    def begin(field):
        for side, ats in ((RIGHT, firsts), (LEFT, seconds)):
            local(field, 0, ats)
            finish(field, 0, ats)
            send_halo(field, 1, side)
        local(field, 1, everyone)

    def one_side(field, level, side):
        wait_halo(field, level, side)
        finish(field, level, firsts if side == LEFT else seconds)
        send_halo(field, level + 1, 1 - side)

    def go_on(field, level):
        for side in (LEFT, RIGHT):
            one_side(field, level, side)
        local(field, level + 1, everyone if level + 1 < last else seconds)

    @when_second
    def _():
        pair_copy(2).wait_recv()
        wait_out(SRC)
        for at in everyone:
            waves[0, SRC, REACH + at, inside, :] = arrived_rows(SRC, 0, at)
        begin(SRC)

    advance_rcv(1)

    @when_second
    def _():
        for index in range(2):
            pair_copy(index).wait_recv()
        for side in (LEFT, RIGHT):
            wait_halo(ALT, 0, side)
        wait_out(ALT)
        for at in everyone:
            for part in range(PARTS):
                medium_alt[part, at] = arrived_rows(ALT, part, at)
        begin(ALT)
        pair_copy(3).start()

    for level in range(1, last):

        @when_second
        def _():
            go_on(SRC, level)

        @when_second
        def _():
            go_on(ALT, level)
            if level + 1 == last - 1:
                pair_copy(4).start()
            if level + 1 == last:
                pair_copy(5).start()

        advance_rcv(level + 1)
    @when_first
    def _():
        for index in (3, 4):
            pair_copy(index).wait_recv()

    keep_src(2)
    keep_rcv(2)
    keep_rcv(steps)
    correlate(0)
    for at in range(slab):
        rcv_next[at] = echoes[steps, REACH + at, inside, :]
        rcv_prior[at] = echoes[last, REACH + at, inside, :]

    @when_first
    def _():
        pair_copy(5).wait_recv()
        local_both(last, firsts)

    def arrive(field):
        @when_second
        def _():
            wait_halo(field, last, RIGHT)
            finish(field, last, seconds)

        @when_first
        def _():
            wait_halo(field, last, LEFT)
            finish(field, last, firsts)

    arrive(SRC)
    keep_src(steps)
    correlate(1)
    arrive(ALT)
    for at in range(slab):
        src_next[at] = waves[steps, ALT, REACH + odd * slab + at, inside, :]
        src_prior[at] = waves[last, ALT, REACH + odd * slab + at, inside, :]

    @when_first
    def _():
        for field in FIELDS:
            sent = staged.at[field, pl.ds(0, pairs * block)]
            pltpu.make_async_copy(sent, sent, out_send.at[field]).wait()
        wait_sent(ALT, 0, RIGHT)
        for index in range(3):
            pair_copy(index).wait_send()

    @when_second
    def _():
        for field in FIELDS:
            sent = staged.at[field, pl.ds(0, (pairs - 1) * block)]
            pltpu.make_async_copy(sent, sent, out_send.at[field]).wait()
        wait_sent(ALT, 0, LEFT)
        for level in range(1, steps):
            for field in FIELDS:
                for side in (LEFT, RIGHT):
                    wait_sent(field, level, side)
        for index in range(3, 6):
            pair_copy(index).wait_send()

    for level in range(steps):
        each_side(lambda side: echo_copy(level, side).wait_send())


def deliver_kernel(*refs):
    count = (len(refs) - 1) // 2
    copies = [
        pltpu.make_async_copy(refs[i], refs[count + i], refs[-1].at[i]) for i in range(count)
    ]
    for copy in copies:
        copy.start()
    for copy in copies:
        copy.wait()


def solution(mesh):
    devices = mesh.shape["wide"]

    def on_device(
        src_now, src_old, rcv_now, rcv_old, medium, wavelet, shot, traces, rec_x, lag_order
    ):
        slab, cells, cells_z = src_now.shape
        assert rcv_now.shape == (slab, cells_z, cells) and slab >= REACH
        assert slab * devices == cells and devices % 2 == 0
        steps = wavelet.shape[0]
        lags = lag_order.shape[0]
        half = (lags - 1) // 2
        rows = 2 * PARTS * slab
        f32 = jnp.float32
        vmem = pl.BlockSpec(memory_space=pltpu.VMEM)
        hbm = pl.BlockSpec(memory_space=pltpu.HBM)
        field_shape = jax.ShapeDtypeStruct((slab, cells, cells_z), f32)
        board_shape = jax.ShapeDtypeStruct((lags, slab, cells, cells_z), f32)
        shapes = (field_shape,) * 4 + (board_shape,)
        taken = steps // 2
        turn = lambda array: jnp.swapaxes(array, -1, -2)
        like = lambda array: pltpu.VMEM(array.shape, array.dtype)
        scalars = lambda array: pltpu.SMEM(array.shape, array.dtype)
        rcv_now, rcv_old, medium, traces = map(turn, (rcv_now, rcv_old, medium, traces))
        both = 2 * slab
        field = lambda *lead: pltpu.VMEM((*lead, cells, cells_z), f32)
        wide = lambda *lead: pltpu.VMEM((*lead, cells + 2 * EDGE, cells_z), f32)
        scratch = [
            field(both),
            like(rcv_old),
            field(PARTS, both),
            field(PARTS, both),
            scalars(wavelet),
            scalars(shot),
            like(traces),
            like(rec_x),
            scalars(lag_order),
            pltpu.VMEM((taken, 2, slab, cells + 2 * half, cells_z), f32),
            pltpu.VMEM((2, devices // 2 * slab * rows, cells_z), f32),
            pltpu.VMEM((2, devices * slab * rows, cells_z), f32),
            wide(steps + 1, 2, both + 2 * REACH),
            wide(steps + 1, slab + 2 * REACH),
            field(PARTS, both),
            field(slab),
            field(steps, slab),
            field(2),
        ]
        held = sum(4 * math.prod(each.shape) for each in scratch + list(shapes))
        results = pl.pallas_call(
            functools.partial(window_kernel, devices),
            out_shape=shapes,
            in_specs=[hbm] * 10,
            out_specs=(vmem,) * 5,
            scratch_shapes=scratch
            + [pltpu.SemaphoreType.DMA((2,))] * 2
            + [pltpu.SemaphoreType.DMA((2, steps, 2))] * 2
            + [pltpu.SemaphoreType.DMA((steps, 2))] * 2
            + [pltpu.SemaphoreType.DMA((6,))] * 2
            + [pltpu.SemaphoreType.DMA((10,))],
            compiler_params=pltpu.CompilerParams(
                collective_id=0, has_side_effects=True, vmem_limit_bytes=held + (4 << 20)
            ),
            name="window",
        )(
            *(
                pltpu.with_memory_space_constraint(array, pltpu.HBM)
                for array in (
                    src_now,
                    src_old,
                    rcv_now,
                    rcv_old,
                    medium,
                    wavelet,
                    shot,
                    traces,
                    rec_x,
                    lag_order,
                )
            )
        )
        outs = pl.pallas_call(
            deliver_kernel,
            out_shape=shapes,
            in_specs=[vmem] * 5,
            out_specs=(hbm,) * 5,
            scratch_shapes=[pltpu.SemaphoreType.DMA((5,))],
            compiler_params=pltpu.CompilerParams(vmem_limit_bytes=held + (4 << 20)),
            name="deliver",
        )(*results)
        return outs[0], outs[1], turn(outs[2]), turn(outs[3]), turn(outs[4])

    return jax.shard_map(
        on_device,
        mesh=mesh,
        in_specs=(
            P("wide", "shots", None),
            P("wide", "shots", None),
            P("wide", "shots", None),
            P("wide", "shots", None),
            P(None, "wide", None, None),
            P(),
            P("shots"),
            P("wide", "shots", None),
            P("wide", "shots"),
            P(),
        ),
        out_specs=(
            P("wide", "shots", None),
            P("wide", "shots", None),
            P("wide", "shots", None),
            P("wide", "shots", None),
            P("shots", "wide", None, None),
        ),
        check_vma=False,
    )
```

```python
import functools
import math

import jax
import jax.numpy as jnp
from jax import lax
from jax.experimental import pallas as pl
from jax.experimental.pallas import tpu as pltpu
from jax.sharding import PartitionSpec as P

REACH = 2
EDGE = 8
OUTER, INNER, CENTRE = -1.0 / 12.0, 4.0 / 3.0, -2.5
SRC, ALT = 0, 1
FIELDS = (SRC, ALT)
PARTS = 3
LEFT, RIGHT = 0, 1
MESH = pl.DeviceIdType.MESH


def second(window):
    return (
        OUTER * (window(-2) + window(2)) + INNER * (window(-1) + window(1)) + CENTRE * window(0)
    )


def window_kernel(
    devices,
    src_now_in,
    src_old_in,
    rcv_now_in,
    rcv_old_in,
    medium_in,
    wavelet_in,
    shot_in,
    traces_in,
    rec_x_in,
    lag_order_in,
    src_next,
    src_prior,
    rcv_next,
    rcv_prior,
    board,
    src_old,
    rcv_old,
    medium,
    medium_alt,
    wavelet,
    shot,
    traces,
    rec_x,
    lag_order,
    padded,
    staged,
    landed,
    waves,
    echoes,
    partial,
    partial_rcv,
    surface,
    columns,
    out_send,
    out_recv,
    halo_send,
    halo_recv,
    echo_send,
    echo_recv,
    pair_send,
    pair_recv,
    load_sems,
):
    me = lax.axis_index("wide")
    pairs = devices // 2
    pair = me // 2
    odd = lax.rem(me, 2)
    slab, cells, cells_z = rcv_old.shape
    both = 2 * slab
    steps = wavelet.shape[0]
    last = steps - 1
    rows = PARTS * both
    block = slab * rows
    inside = pl.ds(EDGE, cells)
    mine = pl.ds(odd * slab, slab)
    mine_waves = pl.ds(REACH + odd * slab, slab)
    own_echoes = pl.ds(REACH, slab)

    lags = lag_order.shape[0]
    half = (lags - 1) // 2
    far_first = sorted(range(1, devices), key=lambda distance: abs(distance - devices // 2))
    far_pairs = sorted(range(1, pairs), key=lambda distance: abs(distance - pairs // 2))

    def when_first(act):
        pl.when(odd == 0)(act)

    def when_second(act):
        pl.when(odd == 1)(act)

    loads = []
    for index, (source, target) in enumerate(
        (
            (src_now_in, waves.at[0, ALT, mine_waves, inside]),
            (src_old_in, src_old.at[mine]),
            (medium_in, medium.at[:, mine]),
            (rcv_now_in, echoes.at[0, own_echoes, inside]),
            (shot_in, shot),
            (traces_in, traces),
            (rec_x_in, rec_x),
            (rcv_old_in, rcv_old),
            (wavelet_in, wavelet),
            (lag_order_in, lag_order),
        )
    ):
        loads.append(pltpu.make_async_copy(source, target, load_sems.at[index]))
    for load in loads[:3]:
        load.start()

    barrier = pltpu.get_barrier_semaphore()

    def greet(peer):
        pl.semaphore_signal(
            barrier, inc=1, device_id={"wide": peer}, device_id_type=MESH
        )

    @when_second
    def _():
        for distance in far_first:
            greet(lax.rem(me + distance, devices))

    @when_first
    def _():
        greet(me + 1)
        pl.when(pair > 0)(lambda: greet(me - 1))

    for load in loads[3:]:
        load.start()

    zero_edge = jnp.zeros((EDGE, cells_z), jnp.float32)
    zero_plane = jnp.zeros((cells, cells_z), jnp.float32)
    zero_half = jnp.zeros((half, cells_z), jnp.float32)

    for at in range(REACH, REACH + both):
        waves[0, ALT, at, 0:EDGE, :] = zero_edge
        waves[0, ALT, at, EDGE + cells : EDGE + cells + EDGE, :] = zero_edge

    row_at = lax.broadcasted_iota(jnp.int32, (cells, cells_z), 0)
    lane_at = lax.broadcasted_iota(jnp.int32, (cells, cells_z), 1)

    def along_rows(plane):
        def window(shift):
            return plane(pl.ds(EDGE + shift, cells))

        return second(window)

    for load in loads[:2]:
        load.wait()
    for at in range(slab):
        def now_rows(where):
            return waves[0, ALT, REACH + odd * slab + at, where, :]

        sent_rows = (
            lambda: now_rows(inside),
            lambda: src_old[odd * slab + at],
            lambda: along_rows(now_rows),
        )
        for part, rows_of in enumerate(sent_rows):
            partial[part, at] = rows_of()
            for y in range(both):
                into = at * rows + part * both + y
                staged[SRC, pl.ds(into, pairs, stride=block), :] = partial[
                    part, at, pl.ds(y, pairs, stride=both), :
                ]

    pl.semaphore_wait(barrier, pairs + odd * (pair < pairs - 1).astype(jnp.int32))

    def remote(source, target, send, recv, peer):
        return pltpu.make_async_remote_copy(
            src_ref=source,
            dst_ref=target,
            send_sem=send,
            recv_sem=recv,
            device_id={"wide": peer},
            device_id_type=MESH,
        )

    def out_copy(field, to):
        return remote(
            staged.at[field, pl.ds(pl.multiple_of(to * block, 8), block)],
            landed.at[field, pl.ds(pl.multiple_of(me * block, 8), block)],
            out_send.at[field],
            out_recv.at[field],
            2 * to + 1,
        )

    def pair_copy(index):
        early = index < 3
        source = (
            waves.at[0, ALT, pl.ds(REACH, slab), inside],
            src_old.at[pl.ds(0, slab)],
            medium.at[:, pl.ds(0, slab)],
            medium_alt.at[:, pl.ds(0, slab)],
            waves.at[last - 1, :, pl.ds(REACH, slab), inside],
            waves.at[last, :, pl.ds(REACH, both), inside],
        )[index]
        peer = 2 * pair + 1 if early else 2 * pair
        return remote(source, source, pair_send.at[index], pair_recv.at[index], peer)

    def halo_copy(field, level, side):
        first = both if side == LEFT else REACH
        into = 0 if side == LEFT else REACH + both
        to = pair + 1 if side == LEFT else pair - 1
        peer = 2 * to if level == last and side == LEFT else 2 * to + 1
        return remote(
            waves.at[level, field, pl.ds(first, REACH), inside],
            waves.at[level, field, pl.ds(into, REACH), inside],
            halo_send.at[field, level, side],
            halo_recv.at[field, level, side],
            peer,
        )

    def sends_to(side):
        return pair < pairs - 1 if side == LEFT else pair > 0

    def gets_from(side):
        return pair > 0 if side == LEFT else pair < pairs - 1

    def send_halo(field, level, side):
        pl.when(sends_to(side))(lambda: halo_copy(field, level, side).start())

    def wait_sent(field, level, side):
        pl.when(sends_to(side))(lambda: halo_copy(field, level, side).wait_send())

    def wait_halo(field, level, side):
        pl.when(gets_from(side))(lambda: halo_copy(field, level, side).wait_recv())

    def echo_copy(level, side):
        first = slab if side == LEFT else REACH
        into = 0 if side == LEFT else REACH + slab
        return remote(
            echoes.at[level, pl.ds(first, REACH), inside],
            echoes.at[level, pl.ds(into, REACH), inside],
            echo_send.at[level, side],
            echo_recv.at[level, side],
            me + 1 if side == LEFT else me - 1,
        )

    def each_side(act):
        pl.when(me < devices - 1)(lambda: act(LEFT))
        pl.when(me > 0)(lambda: act(RIGHT))

    def send_echo(level):
        each_side(lambda side: echo_copy(level, side).start())

    def wait_echo(level):
        each_side(lambda side: echo_copy(level, 1 - side).wait_recv())

    loads[3].wait()
    send_echo(0)

    def send_out(field):
        for distance in far_pairs[::-1]:
            out_copy(field, lax.rem(pair + distance, pairs)).start()

    send_out(SRC)
    loads[2].wait()
    for at in range(slab):
        for part in range(PARTS):
            for x in range(both):
                into = at * rows + part * both + x
                staged[ALT, pl.ds(into, pairs, stride=block), :] = medium[
                    part, odd * slab + at, pl.ds(x, pairs, stride=both), :
                ]
    send_out(ALT)

    for field in FIELDS:
        for level in range(steps):
            for at in range(REACH, REACH + both):
                waves[level, field, at, 0:EDGE, :] = zero_edge
                waves[level, field, at, EDGE + cells : EDGE + cells + EDGE, :] = zero_edge
    for level in range(steps):
        for at in range(REACH, REACH + slab):
            echoes[level, at, 0:EDGE, :] = zero_edge
            echoes[level, at, EDGE + cells : EDGE + cells + EDGE, :] = zero_edge

    for load in loads[4:]:
        load.wait()

    @when_first
    def _():
        for field in FIELDS:
            out_copy(field, pair).start()
        send_halo(ALT, 0, RIGHT)
        for index in range(3):
            pair_copy(index).start()

    @when_second
    def _():
        send_halo(ALT, 0, LEFT)
        own = pl.ds(pl.multiple_of(me * block, 8), block)
        for field in FIELDS:
            landed[field, own, :] = staged[
                field, pl.ds(pl.multiple_of(pair * block, 8), block), :
            ]


    def clear_planes(first):
        for level in range(steps):
            for field in FIELDS:
                for at in range(REACH):
                    waves[level, field, first + at, inside, :] = zero_plane

    pl.when(pair == 0)(lambda: clear_planes(0))
    pl.when(pair == pairs - 1)(lambda: clear_planes(REACH + both))

    def clear_echoes(first):
        for level in range(steps):
            for at in range(REACH):
                echoes[level, first + at, inside, :] = zero_plane

    pl.when(me == 0)(lambda: clear_echoes(0))
    pl.when(me == devices - 1)(lambda: clear_echoes(REACH + slab))

    deep = lane_at == shot[2]
    columns[SRC] = ((row_at == shot[0]) & deep).astype(jnp.float32)
    columns[ALT] = ((row_at == shot[1]) & deep).astype(jnp.float32)
    x_at = lax.broadcasted_iota(jnp.int32, (cells, traces.shape[2]), 0)
    for y in range(slab):
        onehot = (x_at == rec_x[y : y + 1, :]).astype(jnp.float32)
        for step in range(steps):
            total = jnp.sum(onehot * traces[y, step : step + 1, :], axis=1, keepdims=True)
            surface[step, y] = jnp.where(lane_at == 0, total, 0.0)

    def arrived_rows(field, part, at):
        return landed[field, pl.ds(part * both + at, cells, stride=rows), :]

    def along_lanes(centre):
        def window(shift):
            if shift == 0:
                return centre
            turned = pltpu.roll(centre, (-shift) % cells_z, 1)
            kept = lane_at >= -shift if shift < 0 else lane_at < cells_z - shift
            return jnp.where(kept, turned, 0.0)

        return second(window)

    def flat(plane, older, rows_speed, lanes_speed):
        centre = plane(inside)
        return (
            2.0 * centre
            - older
            + rows_speed * along_rows(plane)
            + lanes_speed * along_lanes(centre)
        )

    def speed(field, part, at):
        if field == ALT:
            return medium_alt[part, at]
        return medium[(1, 0, 2)[part], at]

    def local(field, level, ats):
        for at in ats:
            def plane(where):
                return waves[level, field, REACH + at, where, :]

            if level > 0:
                older = waves[level - 1, field, REACH + at, inside, :]
            elif field == ALT:
                older = src_old[at]
            else:
                older = arrived_rows(SRC, 1, at)
            partial[field, at] = flat(plane, older, speed(field, 1, at), speed(field, 2, at))

    def finish(field, level, ats):
        for at in ats:
            def along_planes(shift):
                return waves[level, field, REACH + at + shift, inside, :]

            if field == SRC and level == 0:
                bend = arrived_rows(SRC, 2, at)
            else:
                bend = second(along_planes)
            hit = (pair * both + at == shot[1 if field == SRC else 0]).astype(jnp.float32)
            waves[level + 1, field, REACH + at, inside, :] = (
                partial[field, at]
                + speed(field, 0, at) * bend
                - (wavelet[level] * hit) * columns[field]
            )

    def local_both(level, ats):
        for field in FIELDS:
            local(field, level, ats)

    def local_rcv(level):
        for at in range(slab):
            def plane(where):
                return echoes[level, REACH + at, where, :]

            older = echoes[level - 1, REACH + at, inside, :] if level > 0 else rcv_old[at]
            here = odd * slab + at
            partial_rcv[at] = flat(plane, older, medium[0, here], medium[2, here])

    def finish_rcv(level):
        for at in range(slab):
            def along_planes(shift):
                return echoes[level, REACH + at + shift, inside, :]

            echoes[level + 1, REACH + at, inside, :] = (
                partial_rcv[at]
                + medium[1, odd * slab + at] * second(along_planes)
                + surface[level, at]
            )

    def keep_src(level):
        for y in range(slab):
            padded[level // 2 - 1, 0, y, half : half + cells, :] = waves[
                level, SRC, REACH + odd * slab + y, inside, :
            ]

    def keep_rcv(level):
        for y in range(slab):
            padded[level // 2 - 1, 1, y, half : half + cells, :] = echoes[
                level, REACH + y, inside, :
            ]

    def correlate(snap):
        for plane in range(lags):
            slot = lag_order[plane]
            at_src = pl.ds(2 * half - slot, cells)
            at_rcv = pl.ds(slot, cells)
            for y in range(slab):
                product = padded[snap, 0, y, at_src, :] * padded[snap, 1, y, at_rcv, :]
                board[plane, y] = product if snap == 0 else board[plane, y] + product

    everyone = range(both)
    firsts, seconds = range(slab), range(slab, both)

    def advance_rcv(level):
        wait_echo(level)
        finish_rcv(level)
        if level < last:
            send_echo(level + 1)
            local_rcv(level + 1)

    local_rcv(0)
    advance_rcv(0)
    for snap in range(padded.shape[0]):
        for field in range(2):
            for y in range(slab):
                padded[snap, field, y, 0:half, :] = zero_half
                padded[snap, field, y, half + cells : 2 * half + cells, :] = zero_half

    def wait_out(field):
        arrived = landed.at[field, pl.ds(0, (devices - 1) * block)]
        pltpu.make_async_copy(arrived, arrived, out_recv.at[field]).wait()

    def begin(field):
        for side, ats in ((RIGHT, firsts), (LEFT, seconds)):
            local(field, 0, ats)
            finish(field, 0, ats)
            send_halo(field, 1, side)
        local(field, 1, everyone)

    def one_side(field, level, side):
        wait_halo(field, level, side)
        finish(field, level, firsts if side == LEFT else seconds)
        send_halo(field, level + 1, 1 - side)

    def go_on(field, level):
        for side in (LEFT, RIGHT):
            one_side(field, level, side)
        local(field, level + 1, everyone if level + 1 < last else seconds)

    @when_second
    def _():
        pair_copy(2).wait_recv()
        wait_out(SRC)
        for at in everyone:
            waves[0, SRC, REACH + at, inside, :] = arrived_rows(SRC, 0, at)
        begin(SRC)

    advance_rcv(1)

    @when_second
    def _():
        for index in range(2):
            pair_copy(index).wait_recv()
        for side in (LEFT, RIGHT):
            wait_halo(ALT, 0, side)
        wait_out(ALT)
        for at in everyone:
            for part in range(PARTS):
                medium_alt[part, at] = arrived_rows(ALT, part, at)
        begin(ALT)
        pair_copy(3).start()

    for level in range(1, last):

        @when_second
        def _():
            go_on(SRC, level)

        @when_second
        def _():
            go_on(ALT, level)
            if level + 1 == last - 1:
                pair_copy(4).start()
            if level + 1 == last:
                pair_copy(5).start()

        advance_rcv(level + 1)
    @when_first
    def _():
        for index in (3, 4):
            pair_copy(index).wait_recv()

    keep_src(2)
    keep_rcv(2)
    keep_rcv(steps)
    correlate(0)
    for at in range(slab):
        rcv_next[at] = echoes[steps, REACH + at, inside, :]
        rcv_prior[at] = echoes[last, REACH + at, inside, :]

    @when_first
    def _():
        pair_copy(5).wait_recv()
        local_both(last, firsts)

    def arrive(field):
        @when_second
        def _():
            wait_halo(field, last, RIGHT)
            finish(field, last, seconds)

        @when_first
        def _():
            wait_halo(field, last, LEFT)
            finish(field, last, firsts)

    arrive(SRC)
    keep_src(steps)
    correlate(1)
    arrive(ALT)
    for at in range(slab):
        src_next[at] = waves[steps, ALT, REACH + odd * slab + at, inside, :]
        src_prior[at] = waves[last, ALT, REACH + odd * slab + at, inside, :]

    @when_first
    def _():
        for field in FIELDS:
            sent = staged.at[field, pl.ds(0, pairs * block)]
            pltpu.make_async_copy(sent, sent, out_send.at[field]).wait()
        wait_sent(ALT, 0, RIGHT)
        for index in range(3):
            pair_copy(index).wait_send()

    @when_second
    def _():
        for field in FIELDS:
            sent = staged.at[field, pl.ds(0, (pairs - 1) * block)]
            pltpu.make_async_copy(sent, sent, out_send.at[field]).wait()
        wait_sent(ALT, 0, LEFT)
        for level in range(1, steps):
            for field in FIELDS:
                for side in (LEFT, RIGHT):
                    wait_sent(field, level, side)
        for index in range(3, 6):
            pair_copy(index).wait_send()

    for level in range(steps):
        each_side(lambda side: echo_copy(level, side).wait_send())


def deliver_kernel(*refs):
    count = (len(refs) - 1) // 2
    copies = [
        pltpu.make_async_copy(refs[i], refs[count + i], refs[-1].at[i]) for i in range(count)
    ]
    for copy in copies:
        copy.start()
    for copy in copies:
        copy.wait()


def solution(mesh):
    devices = mesh.shape["wide"]

    def on_device(
        src_now, src_old, rcv_now, rcv_old, medium, wavelet, shot, traces, rec_x, lag_order
    ):
        slab, cells, cells_z = src_now.shape
        assert rcv_now.shape == (slab, cells_z, cells) and slab >= REACH
        assert slab * devices == cells and devices % 2 == 0
        steps = wavelet.shape[0]
        lags = lag_order.shape[0]
        half = (lags - 1) // 2
        rows = 2 * PARTS * slab
        f32 = jnp.float32
        vmem = pl.BlockSpec(memory_space=pltpu.VMEM)
        hbm = pl.BlockSpec(memory_space=pltpu.HBM)
        field_shape = jax.ShapeDtypeStruct((slab, cells, cells_z), f32)
        board_shape = jax.ShapeDtypeStruct((lags, slab, cells, cells_z), f32)
        shapes = (field_shape,) * 4 + (board_shape,)
        taken = steps // 2
        turn = lambda array: jnp.swapaxes(array, -1, -2)
        like = lambda array: pltpu.VMEM(array.shape, array.dtype)
        scalars = lambda array: pltpu.SMEM(array.shape, array.dtype)
        rcv_now, rcv_old, medium, traces = map(turn, (rcv_now, rcv_old, medium, traces))
        both = 2 * slab
        field = lambda *lead: pltpu.VMEM((*lead, cells, cells_z), f32)
        wide = lambda *lead: pltpu.VMEM((*lead, cells + 2 * EDGE, cells_z), f32)
        scratch = [
            field(both),
            like(rcv_old),
            field(PARTS, both),
            field(PARTS, both),
            scalars(wavelet),
            scalars(shot),
            like(traces),
            like(rec_x),
            scalars(lag_order),
            pltpu.VMEM((taken, 2, slab, cells + 2 * half, cells_z), f32),
            pltpu.VMEM((2, devices // 2 * slab * rows, cells_z), f32),
            pltpu.VMEM((2, devices * slab * rows, cells_z), f32),
            wide(steps + 1, 2, both + 2 * REACH),
            wide(steps + 1, slab + 2 * REACH),
            field(PARTS, both),
            field(slab),
            field(steps, slab),
            field(2),
        ]
        held = sum(4 * math.prod(each.shape) for each in scratch + list(shapes))
        results = pl.pallas_call(
            functools.partial(window_kernel, devices),
            out_shape=shapes,
            in_specs=[hbm] * 10,
            out_specs=(vmem,) * 5,
            scratch_shapes=scratch
            + [pltpu.SemaphoreType.DMA((2,))] * 2
            + [pltpu.SemaphoreType.DMA((2, steps, 2))] * 2
            + [pltpu.SemaphoreType.DMA((steps, 2))] * 2
            + [pltpu.SemaphoreType.DMA((6,))] * 2
            + [pltpu.SemaphoreType.DMA((10,))],
            compiler_params=pltpu.CompilerParams(
                collective_id=0, has_side_effects=True, vmem_limit_bytes=held + (4 << 20)
            ),
            name="window",
        )(
            *(
                pltpu.with_memory_space_constraint(array, pltpu.HBM)
                for array in (
                    src_now,
                    src_old,
                    rcv_now,
                    rcv_old,
                    medium,
                    wavelet,
                    shot,
                    traces,
                    rec_x,
                    lag_order,
                )
            )
        )
        outs = pl.pallas_call(
            deliver_kernel,
            out_shape=shapes,
            in_specs=[vmem] * 5,
            out_specs=(hbm,) * 5,
            scratch_shapes=[pltpu.SemaphoreType.DMA((5,))],
            compiler_params=pltpu.CompilerParams(vmem_limit_bytes=held + (4 << 20)),
            name="deliver",
        )(*results)
        return outs[0], outs[1], turn(outs[2]), turn(outs[3]), turn(outs[4])

    return jax.shard_map(
        on_device,
        mesh=mesh,
        in_specs=(
            P("wide", "shots", None),
            P("wide", "shots", None),
            P("wide", "shots", None),
            P("wide", "shots", None),
            P(None, "wide", None, None),
            P(),
            P("shots"),
            P("wide", "shots", None),
            P("wide", "shots"),
            P(),
        ),
        out_specs=(
            P("wide", "shots", None),
            P("wide", "shots", None),
            P("wide", "shots", None),
            P("wide", "shots", None),
            P("shots", "wide", None, None),
        ),
        check_vma=False,
    )
```
